32 devices in a mesh: exp: 4 (over z), row: 2 (over core), basis: 4 (over y, x).
Axes of the slice: x: 2, y: 2, z: 4, core: 2. Of those that a mesh axis runs over, the one named last changes fastest.
Arguments:
- scene_patches: bfloat16 [256, 4096], P(('exp', 'row')), may hold values from -6 to 6
- visit_dest: int32 [256, 4], P(('exp', 'row')), may hold values from 0 to 7, all different within a row; in each aligned block of 32 rows (0 to 31, 32 to 63, ...) at most 32 rows name the same one
- visit_block: int32 [256, 4], P(('exp', 'row')), may hold values from 0 to 127
- row_maps: bfloat16 [16, 96, 64], P('basis'), may hold values from -0.75 to 0.75
- col_maps: bfloat16 [16, 96, 64], P('basis'), may hold values from -0.75 to 0.75
- psf_weights: bfloat16 [32, 16, 4, 8], P('exp', 'basis', 'row'), may hold values from -1.796875 to 1.796875
- inv_variance: float32 [32], P(('exp', 'basis')), may hold values from 0.25 to 1
- observed: bfloat16 [32, 256, 512], P(('exp', 'basis'), 'row'), may hold values from -12 to 12
Outputs:
- residual: float32 [32, 256, 512], P(('exp', 'basis'), 'row')
The draws below stay inside these ranges and needn't reach their ends.
Inputs may be any that keep to these rules, and one draw needn't show every extreme that they name: `visit_dest`: the 4 entries of a patch name different row bands. Among the 32 patches of one device no value is named more than 32 times, a bound that some block reaches.
All inputs are finite; a program needn't handle non-finite values.
Results may differ from the reference program's by a relative error of at most 0.0038.
Values may be sent and summed in bfloat16 or wider, within the bound.
No kernel may reach another device: no remote copies, remote signals or barrier semaphores. Data moves between devices by JAX's collectives and lax.ppermute only.
A program may use at most 64 MiB of HBM per device.

```python
import math
import jax
import jax.numpy as jnp
import numpy as np
from jax import lax

BLOCK = 64
SPILL = 16
BASIS = 16
VISITS = 4
EXP_DEV = 2
BAND_ROWS = 128
TILE_COLS = 512
PATCH_DEV = 32
OUTW = 96
CAP = 32
PATCHES = 256
EXPOSURES = 32
ROWS = 256
GROUP_BLOCKS = 128
N_EXP = 4
N_ROW = 2
N_BASIS = 4


def with_ends(entries, stream_key, low, high):
    dims = entries.shape
    spot = [jax.random.randint(jax.random.fold_in(stream_key, axis), (), 0, dims[axis]) for axis in range(len(dims))]
    entries = entries.at[tuple(spot)].set(low)
    longest = dims.index(max(dims))
    spot[longest] = (spot[longest] + 1) % dims[longest]
    return entries.at[tuple(spot)].set(high)


def block_scale(key, shape, shards, smallest, high):
    factor_of = 1.0
    for axis_at, parts in shards:
        draws = jax.random.uniform(jax.random.fold_in(jax.random.fold_in(key, 6), axis_at), (parts,), jnp.float32, smallest / len(shards), high / len(shards))
        factor_of = factor_of * jnp.repeat(jnp.exp(draws), shape[axis_at] // parts).reshape((-1,) + (1,) * (len(shape) - 1 - axis_at))
    return factor_of


def routed_block(key, own, number, rows, amount, top, reach, slope):
    order = jax.random.permutation(key, amount)
    crowded, usual = portions_of(amount, rows * top, reach, slope, True), portions_of(amount, rows * top, reach, slope, False)
    places = jnp.arange(amount)

    def named(sizes, rotation):
        used = int((sizes > 0).sum())
        fixed = max(1, used // 4)
        shifted = fixed + (places - fixed + rotation * (used - fixed)) % max(1, amount - fixed)
        return jnp.zeros((amount,), jnp.int32).at[order[jnp.where(places < fixed, places, shifted)]].set(jnp.asarray(sizes, jnp.int32))

    sizes = jnp.where(number % 4 == 0, named(crowded, number // 4), named(usual, number - number // 4 - 1))
    mixed = jax.random.permutation(jax.random.fold_in(own, 3), amount)
    donor, sink = mixed[0:amount // 2 * 2:2], mixed[1:amount // 2 * 2:2]
    room = jnp.minimum(sizes[donor] - 1, reach - sizes[sink]) // 2
    room = jnp.where((donor == order[0]) | (sink == order[0]) | (sizes[sink] == 0), 0, jnp.maximum(room, 0))
    shifted = jax.random.randint(jax.random.fold_in(own, 4), (amount // 2,), 0, 1 << 20) % (room + 1)
    sizes = sizes.at[donor].add(-shifted).at[sink].add(shifted)
    labels = jnp.searchsorted(jnp.cumsum(sizes), jnp.arange(rows * top), side="right").astype(jnp.int32)
    grid = labels.reshape(top, rows).T
    grid = grid[jax.random.permutation(jax.random.fold_in(own, 1), rows)]
    rotation = jax.random.randint(jax.random.fold_in(own, 2), (rows, 1), 0, top)
    return jnp.take_along_axis(grid, (jnp.arange(top)[None, :] + rotation) % top, axis=1)


def portions_of(number_of, total, most, lean, full):
    portions = [(1 << 20) // math.isqrt(rank ** lean) + 1 for rank in range(1, number_of + 1)]
    largest = most if full else min(most, max(-(-total // number_of), total * portions[0] // sum(portions)))
    least = 1 if total - largest >= number_of - 1 else 0
    holding, spare = [largest] + [least] * (number_of - 1), total - largest - least * (number_of - 1)
    while spare > 0:
        free = [i for i in range(1, number_of) if holding[i] < largest] or [i for i in range(1, number_of) if holding[i] < most]
        pool, budget = sum([portions[i] for i in free]), spare
        for i in free:
            extra = min(most - holding[i], max(1, budget * portions[i] // pool), spare)
            holding[i] = holding[i] + extra
            spare = spare - extra
    return np.array(holding)


def noise(stream_key, dims, scale, limit, split=(), dtype=jnp.bfloat16):
    values = scale * jax.random.normal(stream_key, dims, jnp.float32)
    if split:
        values = values * block_scale(stream_key, dims, split, -0.22, 0.18)
    return jnp.clip(values, -limit, limit).astype(dtype)


def setup_inputs(seed: int = 0) -> dict:
    arg_keys = jax.random.split(jax.random.key(seed), 9)
    scene_patches = noise(arg_keys[0], (PATCHES, BLOCK * BLOCK), 1.0, 6.0, ((0, 8),))
    visit_dest_keys = jax.random.split(jax.random.fold_in(arg_keys[1], 1), PATCHES // PATCH_DEV)
    visit_dest_turns = jax.random.permutation(jax.random.fold_in(arg_keys[1], 3), PATCHES // PATCH_DEV)
    visit_dest = jax.vmap(lambda own, number: routed_block(jax.random.fold_in(arg_keys[1], 2), own, number, PATCH_DEV, N_EXP * N_ROW, VISITS, CAP, 2))(visit_dest_keys, visit_dest_turns).reshape((PATCHES, VISITS))
    visit_block = with_ends(jax.random.randint(arg_keys[2], (PATCHES, VISITS), 0, GROUP_BLOCKS), jax.random.fold_in(arg_keys[2], 1), 0, GROUP_BLOCKS - 1).astype(jnp.int32)
    row_maps = noise(arg_keys[3], (BASIS, OUTW, BLOCK), BLOCK ** -0.5, 0.75, ((0, 4),))
    col_maps = noise(arg_keys[4], (BASIS, OUTW, BLOCK), BLOCK ** -0.5, 0.75, ((0, 4),))
    psf_weights = noise(arg_keys[5], (EXPOSURES, BASIS, ROWS // BLOCK, TILE_COLS // BLOCK), 0.3, 1.796875, ((0, 4), (1, 4), (2, 2)))
    inv_variance = jnp.clip(jnp.exp(math.log(1.0) - 1.3862944 * jax.random.uniform(arg_keys[6], (EXPOSURES,), jnp.float32) ** block_scale(arg_keys[6], (EXPOSURES,), ((0, 16),), -0.2, 0.2)), 0.25, 1.0)
    observed = noise(arg_keys[7], (EXPOSURES, ROWS, TILE_COLS), 2.0, 12.0, ((0, 16), (1, 2)))
    return {"scene_patches": scene_patches, "visit_dest": visit_dest, "visit_block": visit_block, "row_maps": row_maps, "col_maps": col_maps, "psf_weights": psf_weights, "inv_variance": inv_variance, "observed": observed}


def pad_last(values, lower, upper):
    widths = [(0, 0)] * (values.ndim - 1) + [(lower, upper)]
    return jnp.pad(values, widths)

def fold_last(values, block_size):
    blocks_along = values.shape[-2]
    edge_width = values.shape[-1] - block_size
    lead = values.shape[:-2]
    head_part = values[..., :block_size].reshape(lead + (blocks_along * block_size,))
    tail_part = pad_last(values[..., block_size:], 0, block_size - edge_width)
    tail_part = tail_part.reshape(lead + (blocks_along * block_size,))
    head_part = pad_last(head_part, 0, edge_width)
    tail_part = pad_last(tail_part, block_size, 0)[..., :blocks_along * block_size + edge_width]
    return head_part + tail_part

def fold_blocks(images, block_size):
    images = jnp.swapaxes(images, -3, -2)
    images = fold_last(images, block_size)
    images = jnp.moveaxis(images, -1, -3)
    images = fold_last(images, block_size)
    return jnp.swapaxes(images, -1, -2)

def reference(scene_patches, visit_dest, visit_block, row_maps, col_maps, psf_weights, inv_variance, observed):
    band_grid = BAND_ROWS // BLOCK
    col_grid = TILE_COLS // BLOCK
    row_grid = ROWS // BLOCK
    per_band = band_grid * col_grid
    per_exposure = row_grid * col_grid
    group_exp = EXP_DEV * N_BASIS
    group_index = visit_dest // N_ROW
    band_index = visit_dest % N_ROW
    local_exp = visit_block // per_band
    within = visit_block % per_band
    block_row = band_index * band_grid + within // col_grid
    block_col = within % col_grid
    exposure = group_index * group_exp + local_exp
    block_ids = (exposure * per_exposure + block_row * col_grid + block_col).astype(jnp.int32)
    total_blocks = EXPOSURES * per_exposure
    patch_values = scene_patches.astype(jnp.float32)

    def add_visit(carry, column):
        return (carry + jax.ops.segment_sum(patch_values, column, num_segments=total_blocks), None)
    summed, _ = lax.scan(add_visit, jnp.zeros((total_blocks, BLOCK * BLOCK), jnp.float32), block_ids.T)
    blocks = summed.astype(jnp.bfloat16)
    blocks = lax.optimization_barrier(blocks)
    blocks = blocks.reshape(EXPOSURES, per_exposure, BLOCK, BLOCK)
    col_wide = col_maps.astype(jnp.float32)
    row_wide = row_maps.astype(jnp.float32)

    def per_exp(items):
        tile_blocks, coeffs = items
        smeared = jnp.einsum('nij,kcj->knic', tile_blocks.astype(jnp.float32), col_wide).astype(jnp.bfloat16)
        smeared = lax.optimization_barrier(smeared)
        scales = coeffs.reshape(BASIS, per_exposure).astype(jnp.float32)
        scaled = (scales[:, :, None, None] * smeared.astype(jnp.float32)).astype(jnp.bfloat16)
        scaled = lax.optimization_barrier(scaled)
        images = jnp.einsum('kor,knrc->noc', row_wide, scaled.astype(jnp.float32))
        images = images.reshape(row_grid, col_grid, OUTW, OUTW)
        canvas = fold_blocks(images, BLOCK)
        return canvas[SPILL:SPILL + ROWS, SPILL:SPILL + TILE_COLS]
    model = lax.map(per_exp, (blocks, psf_weights))
    return jnp.sqrt(inv_variance)[:, None, None] * (observed.astype(jnp.float32) - model)
```

```python
import functools
import jax
import jax.numpy as jnp
from jax import lax
from jax.experimental import pallas as pl
from jax.experimental.pallas import tpu as pltpu
from jax.sharding import PartitionSpec as P

LANES = 128
VMEM_BYTES = 28 * 1024 * 1024


def swapped(value, axis, by):
    length = lax.axis_size(axis)
    return lax.ppermute(value, axis, [(i, i ^ by) for i in range(length)])


def in_vmem(count):
    return [pl.BlockSpec(memory_space=pltpu.VMEM)] * count


def visit_codes(tags, visits, group_blocks):
    tags = tags.astype(jnp.float32)
    return tags[:, :visits] * group_blocks + tags[:, visits : 2 * visits]


def picks(tags, dims, places):
    visits, group_blocks, per_exp, col_grid, band_grid, strips, exp_local, rows_axis = dims
    group, band, basis = places
    codes = visit_codes(tags, visits, group_blocks)
    lane = lax.broadcasted_iota(jnp.int32, (1, LANES), 1)
    exp_at = lane // (strips * col_grid)
    strip = lane // col_grid % strips
    block_row = band * (band_grid - 1) + strip
    dest = group * rows_axis + block_row // band_grid
    block = (basis * exp_local + exp_at) * per_exp + block_row % band_grid * col_grid + lane % col_grid
    want = jnp.where(exp_at < exp_local, dest * group_blocks + block, -1).astype(jnp.float32)
    hit = jnp.zeros((tags.shape[0], LANES), jnp.float32)
    for v in range(visits):
        hit = hit + jnp.where(codes[:, v : v + 1] == want, 1.0, 0.0)
    blocks = exp_local * strips * col_grid
    return hit.T[:blocks].astype(jnp.bfloat16)


def summed_into(out_ref, chunk_refs, before_ref, dims, width, blocks):
    places = (lax.axis_index("exp"), lax.axis_index("row"), lax.axis_index("basis"))
    tags = jnp.concatenate([ref[:, width:] for ref in chunk_refs], axis=0)
    pick = picks(tags, dims, places)
    step = 4 * LANES
    for start in range(0, width, step):
        rows = jnp.concatenate([ref[:, start : start + step] for ref in chunk_refs], axis=0)
        part = jnp.dot(pick, rows, preferred_element_type=jnp.float32)
        for t in range(step // LANES):
            at = (start // LANES + t) * blocks
            piece = part[:, t * LANES : (t + 1) * LANES]
            if before_ref is not None:
                piece = piece + before_ref[at : at + blocks, :]
            out_ref[at : at + blocks, :] = piece


def early_kernel(dims, width, block, kinds_local, *refs):
    chunk_count = 6
    chunks = refs[:chunk_count]
    parcels = refs[chunk_count:-5]
    sums_ref, rows_ref, main_ref, edge_ref, wide_ref = refs[-5:]
    visits, group_blocks, per_exp, col_grid, band_grid, strips, exp_local, rows_axis = dims
    blocks = exp_local * strips * col_grid
    summed_into(sums_ref, chunks, None, dims, width, blocks)
    band = lax.axis_index("row")
    out_rows = 96
    kinds = kinds_local * len(parcels)
    src = lax.broadcasted_iota(jnp.int32, (LANES, 2 * LANES), 0)
    dst = lax.broadcasted_iota(jnp.int32, (LANES, 2 * LANES), 1)
    half = block // 2
    inner = dst % block
    wanted = inner % half * 2 + inner // half
    perm = jnp.where((src == wanted) & (dst < strips * block), 1.0, 0.0).astype(jnp.bfloat16)
    lane2 = lax.broadcasted_iota(jnp.int32, (out_rows, 2 * LANES), 1)
    spill = (out_rows - block) // 2
    lane_c = lax.broadcasted_iota(jnp.int32, (block, 2 * LANES), 1)
    lane_e = lax.broadcasted_iota(jnp.int32, (block, LANES), 1)
    for k in range(kinds):
        parcel = parcels[k // kinds_local]
        both = parcel[(k % kinds_local) * out_rows : (k % kinds_local + 1) * out_rows, :]
        moved = jnp.dot(both, perm, preferred_element_type=jnp.float32)
        gap = jnp.zeros((block, 2 * LANES), jnp.float32)
        total = None
        for s in range(strips):
            piece = jnp.where(lane2 // block == s, moved, 0.0)
            parts = [gap] * s + [piece] + [gap] * (strips - 1 - s)
            piece = jnp.concatenate(parts, axis=0)
            total = piece if total is None else total + piece
        first = total[spill : spill + 2 * block, : strips * block]
        second = total[spill + block : spill + 3 * block, : strips * block]
        chosen = jnp.where(band == 0, first, second).astype(jnp.bfloat16)
        rows_ref[k * 2 * block : (k + 1) * 2 * block, :] = chosen
        cols = both.astype(jnp.float32)
        cols = jnp.concatenate([cols, jnp.zeros((LANES - out_rows, LANES), jnp.float32)], axis=0)
        turned = cols.T[block:, :]
        turned = jnp.concatenate([turned, jnp.zeros_like(turned)], axis=1)
        for b in range(4):
            shift = (b * block - spill) % (2 * LANES)
            placed = pltpu.roll(turned, shift, 1)
            kept = placed
            if b == 0:
                kept = jnp.where(lane_c < 2 * LANES - spill, placed, 0.0)
                edge = jnp.where(lane_e >= LANES - spill, placed[:, LANES:], 0.0)
                edge_ref[0, k * LANES : k * LANES + block, :] = edge.astype(jnp.bfloat16)
                edge_ref[0, k * LANES + block : (k + 1) * LANES, :] = jnp.zeros((block, LANES), jnp.bfloat16)
            if b == 3:
                kept = jnp.where(lane_c >= spill, placed, 0.0)
                edge = jnp.where(lane_e < spill, placed[:, :LANES], 0.0)
                edge_ref[1, k * LANES + block : (k + 1) * LANES, :] = edge.astype(jnp.bfloat16)
                edge_ref[1, k * LANES : k * LANES + block, :] = jnp.zeros((block, LANES), jnp.bfloat16)
            at = k * 4 * block + b * block
            main_ref[at : at + block, :] = kept.astype(jnp.bfloat16)
    src = lax.broadcasted_iota(jnp.int32, (LANES, col_grid * block), 0)
    dst = lax.broadcasted_iota(jnp.int32, (LANES, col_grid * block), 1)
    spread = jnp.where(src == dst // block, 1.0, 0.0).astype(jnp.bfloat16)
    for p, parcel in enumerate(parcels):
        table = parcel[kinds_local * out_rows :, :]
        lines = jnp.dot(table, spread, preferred_element_type=jnp.float32)
        for x in range(exp_local):
            for s in range(strips):
                for kl in range(kinds_local):
                    line = (x * (strips + 1) + s) * kinds_local + kl
                    wide = jnp.broadcast_to(lines[line : line + 1], (16, col_grid * block))
                    at = ((x * kinds + p * kinds_local + kl) * strips + s) * 16
                    wide_ref[at : at + 16, :] = wide.astype(jnp.bfloat16)


def late_kernel(dims, width, block, kinds, *refs):
    chunks = refs[:6]
    (before_ref, rows_ref, main_ref, edge_ref, wide_ref, obs_ref, inv_ref, out_ref) = refs[6:14]
    sums_ref, image_ref, mid_ref, side_ref = refs[14:]
    visits, group_blocks, per_exp, col_grid, band_grid, strips, exp_local, rows_axis = dims
    blocks = exp_local * strips * col_grid
    summed_into(sums_ref, chunks, before_ref, dims, width, blocks)
    half = block // 2
    low = lax.broadcasted_iota(jnp.int32, (half, LANES), 1) < block
    tall = strips * block
    wide_cols = col_grid * block
    band_rows = band_grid * block
    for x in range(exp_local):
        for s in range(strips):
            for m in range(col_grid // 2):
                n = (x * strips + s) * col_grid + 2 * m
                a = sums_ref[pl.ds(n, half, stride=blocks), :]
                b = sums_ref[pl.ds(n + 1, half, stride=blocks), :]
                even = jnp.where(low, a, pltpu.roll(b, block, 1))
                odd = jnp.where(low, pltpu.roll(a, block, 1), b)
                at = s * block
                cols = slice(m * LANES, (m + 1) * LANES)
                image_ref[x, at : at + half, cols] = even.astype(jnp.bfloat16)
                image_ref[x, at + half : at + block, cols] = odd.astype(jnp.bfloat16)
    window = 4 * block
    for x in range(exp_local):
        for k in range(kinds):
            image = image_ref[x].reshape(strips, block // 16, 16, wide_cols)
            at = (x * kinds + k) * strips * 16
            wide = wide_ref[at : at + strips * 16, :].reshape(strips, 1, 16, wide_cols)
            scaled = (image * wide).reshape(tall, wide_cols)
            rows = rows_ref[k * band_rows : (k + 1) * band_rows, :]
            mid = jnp.dot(rows, scaled, preferred_element_type=jnp.float32).astype(jnp.bfloat16)
            for w in range(2):
                top = (w * exp_local + x) * band_rows
                mid_ref[top : top + band_rows, k * window : (k + 1) * window] = mid[:, w * window : (w + 1) * window]
            at = x * band_rows
            cols = slice(k * LANES, (k + 1) * LANES)
            side_ref[0, at : at + band_rows, cols] = mid[:, window : window + LANES]
            side_ref[1, at : at + band_rows, cols] = mid[:, window - LANES : window]
    tall2 = exp_local * band_rows
    for w in range(2):
        main = jnp.dot(mid_ref[w * tall2 : (w + 1) * tall2, :], main_ref[...], preferred_element_type=jnp.float32)
        side = jnp.dot(side_ref[w], edge_ref[w], preferred_element_type=jnp.float32)
        for x in range(exp_local):
            rows = slice(x * band_rows, (x + 1) * band_rows)
            noise = jnp.sqrt(jnp.full((1, LANES), inv_ref[x], jnp.float32))
            for t in range(2):
                model = main[rows, t * LANES : (t + 1) * LANES]
                if t == 1 - w:
                    model = model + side[rows]
                cols = slice(w * window + t * LANES, w * window + (t + 1) * LANES)
                out_ref[x, :, cols] = noise * (obs_ref[x, :, cols].astype(jnp.float32) - model)


def gathered_device(
    scene_patches, visit_dest, visit_block, row_maps, col_maps, psf_weights, inv_variance, observed
):
    n_exp, n_row, n_basis = (lax.axis_size(a) for a in ("exp", "row", "basis"))
    patch_count, visits = visit_dest.shape
    width = scene_patches.shape[1]
    exp_local, band_rows, tile_cols = observed.shape
    exp_group, kinds_local, band_grid, col_grid = psf_weights.shape
    block = row_maps.shape[2]
    out_width = row_maps.shape[1]
    strips = band_grid + 1
    per_exp = band_grid * col_grid
    group_blocks = exp_group * per_exp
    kinds = kinds_local * n_basis
    basis, band = lax.axis_index("basis"), lax.axis_index("row")
    dims = (visits, group_blocks, per_exp, col_grid, band_grid, strips, exp_local, n_row)
    blocks = exp_local * strips * col_grid

    tags = jnp.concatenate([visit_dest, visit_block], axis=1).astype(jnp.bfloat16)
    tags = jnp.pad(tags, ((0, 0), (0, LANES - 2 * visits)))
    own = jnp.concatenate([scene_patches, tags], axis=1)
    part = patch_count // n_basis
    own_part = lax.dynamic_slice_in_dim(own, basis * part, part, 0)

    far = [swapped(own_part, "exp", s) for s in range(n_exp - 1, 1, -1)]
    near = swapped(own, "exp", 1)
    own_other = swapped(own, "row", 1)

    weights_other = swapped(psf_weights, "row", 1)
    weights = jnp.where(
        band == 0,
        jnp.concatenate([psf_weights, weights_other[:, :, :1]], axis=2),
        jnp.concatenate([weights_other[:, :, band_grid - 1 :], psf_weights], axis=2),
    )
    weights = jnp.pad(jnp.swapaxes(weights, 1, 2), ((0, 0), (0, 1), (0, 0), (0, LANES - col_grid)))
    weights = weights.reshape(n_basis, -1, LANES)
    maps = jnp.concatenate([row_maps, col_maps], axis=2).reshape(-1, LANES)
    parcels = []
    for s in range(n_basis):
        table = lax.dynamic_index_in_dim(weights, basis ^ s, 0, keepdims=False)
        parcel = jnp.concatenate([maps, table], axis=0)
        parcels.append(swapped(parcel, "basis", s) if s else parcel)

    far = jnp.concatenate(far, axis=0)
    spread = [swapped(far, "basis", s) for s in range(n_basis - 1, 0, -1)]
    near_other = swapped(near, "row", 1)
    far_other = swapped(far, "row", 1)
    spread_other = [swapped(v, "row", 1) for v in spread]

    f32, bf16 = jnp.float32, jnp.bfloat16
    params = pltpu.CompilerParams(vmem_limit_bytes=VMEM_BYTES)
    early = [own, near, far, own_other, near_other, far_other] + parcels
    shapes = [
        jax.ShapeDtypeStruct((width // LANES * blocks, LANES), f32),
        jax.ShapeDtypeStruct((kinds * band_rows, strips * block), bf16),
        jax.ShapeDtypeStruct((kinds * 4 * block, 4 * block), bf16),
        jax.ShapeDtypeStruct((2, kinds * LANES, LANES), bf16),
        jax.ShapeDtypeStruct((exp_local * kinds * strips * 16, tile_cols), bf16),
    ]
    tables = pl.pallas_call(
        functools.partial(early_kernel, dims, width, block, kinds_local),
        out_shape=shapes,
        in_specs=in_vmem(len(early)),
        out_specs=in_vmem(len(shapes)),
        compiler_params=params,
    )(*early)
    late = spread + spread_other + list(tables) + [observed]
    return pl.pallas_call(
        functools.partial(late_kernel, dims, width, block, kinds),
        out_shape=jax.ShapeDtypeStruct(observed.shape, f32),
        in_specs=in_vmem(len(late)) + [pl.BlockSpec(memory_space=pltpu.SMEM)],
        out_specs=pl.BlockSpec(memory_space=pltpu.VMEM),
        scratch_shapes=[
            pltpu.VMEM((width // LANES * blocks, LANES), f32),
            pltpu.VMEM((exp_local, strips * block, tile_cols), bf16),
            pltpu.VMEM((2 * exp_local * band_rows, kinds * 4 * block), bf16),
            pltpu.VMEM((2, exp_local * band_rows, kinds * LANES), bf16),
        ],
        compiler_params=params,
    )(*late, inv_variance)


def passed_along(value, axis, by):
    length = lax.axis_size(axis)
    pairs = [(i, i + by) for i in range(length) if 0 <= i + by < length]
    return lax.ppermute(value, axis, pairs)


def pad_last(values, lower, upper):
    widths = [(0, 0)] * (values.ndim - 1) + [(lower, upper)]
    return jnp.pad(values, widths)


def fold_last(values, block_size):
    blocks_along = values.shape[-2]
    edge_width = values.shape[-1] - block_size
    lead = values.shape[:-2]
    head_part = values[..., :block_size].reshape(lead + (blocks_along * block_size,))
    tail_part = pad_last(values[..., block_size:], 0, block_size - edge_width)
    tail_part = tail_part.reshape(lead + (blocks_along * block_size,))
    head_part = pad_last(head_part, 0, edge_width)
    tail_part = pad_last(tail_part, block_size, 0)[..., : blocks_along * block_size + edge_width]
    return head_part + tail_part


def fold_blocks(images, block_size):
    images = jnp.swapaxes(images, -3, -2)
    images = fold_last(images, block_size)
    images = jnp.moveaxis(images, -1, -3)
    images = fold_last(images, block_size)
    return jnp.swapaxes(images, -1, -2)


def band_model(block_rows, weights, row_ops, col_ops, spill_rows, tile_cols):
    count_exp, kind_count, block_grid, col_grid = weights.shape
    block_size = row_ops.shape[2]
    out_width = row_ops.shape[1]
    tile_blocks = block_rows.reshape(-1, block_size, block_size)
    smeared = jnp.einsum(
        "nij,kcj->knic", tile_blocks, col_ops, preferred_element_type=jnp.float32
    ).astype(jnp.bfloat16)
    smeared = lax.optimization_barrier(smeared)
    scales = jnp.swapaxes(weights, 0, 1).reshape(kind_count, -1).astype(jnp.float32)
    scaled = (scales[:, :, None, None] * smeared).astype(jnp.bfloat16)
    images = jnp.einsum("kor,knrc->noc", row_ops, scaled, preferred_element_type=jnp.float32)
    images = images.reshape(count_exp, block_grid, col_grid, out_width, out_width)
    canvas = fold_blocks(images, block_size)
    return canvas[:, :, spill_rows : spill_rows + tile_cols]


def exchanged_device(
    scene_patches, visit_dest, visit_block, row_maps, col_maps, psf_weights, inv_variance, observed
):
    group_size = lax.axis_size("exp") * lax.axis_size("row")
    patch_count, visit_count = visit_dest.shape
    capacity = max(2, 2 * patch_count * visit_count // group_size)
    exp_local, band_rows, tile_cols = observed.shape
    exp_group, kind_count, block_grid, col_grid = psf_weights.shape
    block_size = row_maps.shape[2]
    spill_rows = (row_maps.shape[1] - block_size) // 2
    per_exposure = block_grid * col_grid
    flat_dest = visit_dest.reshape(-1)
    matches = (flat_dest[:, None] == jnp.arange(group_size, dtype=jnp.int32)[None, :]).astype(
        jnp.int32
    )
    slot_rank = jnp.sum(jnp.cumsum(matches, axis=0) * matches, axis=1) - 1
    slot_index = flat_dest * capacity + slot_rank
    select_mat = (
        slot_index[None, :] == jnp.arange(group_size * capacity, dtype=jnp.int32)[:, None]
    ).astype(jnp.int32)
    tagged = jnp.sum(select_mat * (visit_block.reshape(-1) + 1)[None, :], axis=1).astype(
        jnp.bfloat16
    )
    picker = jnp.sum(
        select_mat.reshape(group_size * capacity, patch_count, visit_count), axis=2
    ).astype(jnp.bfloat16)
    outgoing = jnp.dot(picker, scene_patches, preferred_element_type=jnp.float32).astype(
        jnp.bfloat16
    )
    shaped = outgoing.reshape(group_size, capacity, -1)
    labels = tagged.reshape(group_size, capacity)
    arrived, arrived_tags = (
        lax.all_to_all(shaped, ("exp", "row"), split_axis=0, concat_axis=0, tiled=True),
        lax.all_to_all(labels, ("exp", "row"), split_axis=0, concat_axis=0, tiled=True),
    )
    arrived = arrived.reshape(group_size * capacity, -1)
    arrived_tags = arrived_tags.reshape(-1).astype(jnp.int32)
    row_all, col_all, weight_all = (
        lax.all_gather(row_maps, "basis", axis=0, tiled=True),
        lax.all_gather(col_maps, "basis", axis=0, tiled=True),
        lax.all_gather(psf_weights, "basis", axis=1, tiled=True),
    )
    first_exp = lax.axis_index("basis") * exp_local
    wanted = first_exp * per_exposure + 1 + jnp.arange(exp_local * per_exposure, dtype=jnp.int32)
    placing = (arrived_tags[None, :] == wanted[:, None]).astype(jnp.bfloat16)
    own_blocks = jnp.dot(placing, arrived, preferred_element_type=jnp.float32).astype(jnp.bfloat16)
    own_weights = lax.dynamic_slice_in_dim(weight_all, first_exp, exp_local, 0)
    model_band = band_model(own_blocks, own_weights, row_all, col_all, spill_rows, tile_cols)
    upper_spill = model_band[:, :spill_rows]
    lower_spill = model_band[:, spill_rows + band_rows :]
    from_above = passed_along(lower_spill.astype(jnp.bfloat16), "row", 1).astype(lower_spill.dtype)
    from_below = passed_along(upper_spill.astype(jnp.bfloat16), "row", -1).astype(upper_spill.dtype)
    core_rows = model_band[:, spill_rows : spill_rows + band_rows]
    core_rows = core_rows.at[:, :spill_rows].add(from_above)
    core_rows = core_rows.at[:, band_rows - spill_rows :].add(from_below)
    return jnp.sqrt(inv_variance)[:, None, None] * (observed.astype(jnp.float32) - core_rows)


def gathers(mesh, patch_count, visits):
    n_exp, n_row, n_basis = mesh.shape["exp"], mesh.shape["row"], mesh.shape["basis"]
    capacity = max(2, 2 * patch_count * visits // (n_exp * n_row))
    powers = all(n & (n - 1) == 0 for n in (n_exp, n_basis)) and n_exp > 2
    return capacity >= patch_count and powers and n_row == 2 and patch_count % (8 * n_basis) == 0


def per_device(mesh, *arrays):
    patch_count, visits = arrays[1].shape
    if gathers(mesh, patch_count, visits):
        return gathered_device(*arrays)
    return exchanged_device(*arrays)


def solution(mesh):
    return jax.shard_map(
        functools.partial(per_device, mesh),
        mesh=mesh,
        in_specs=(
            P(("exp", "row"), None),
            P(("exp", "row"), None),
            P(("exp", "row"), None),
            P("basis", None, None),
            P("basis", None, None),
            P("exp", "basis", "row", None),
            P(("exp", "basis")),
            P(("exp", "basis"), "row", None),
        ),
        out_specs=P(("exp", "basis"), "row", None),
        check_vma=False,
    )
```

```python
import functools
import jax
import jax.numpy as jnp
from jax import lax
from jax.experimental import pallas as pl
from jax.experimental.pallas import tpu as pltpu
from jax.sharding import PartitionSpec as P


LANES = 128
VMEM_BYTES = 28 * 1024 * 1024


def swapped(value, axis, by):
    length = lax.axis_size(axis)
    return lax.ppermute(value, axis, [(i, i ^ by) for i in range(length)])


def in_vmem(count):
    return [pl.BlockSpec(memory_space=pltpu.VMEM)] * count


def visit_codes(tags, visits, group_blocks):
    tags = tags.astype(jnp.float32)
    return tags[:, :visits] * group_blocks + tags[:, visits : 2 * visits]


def pack_kernel(patch_ref, dest_ref, block_ref, row_ref, col_ref, weight_ref, *refs):
    own_ref, row_out, col_out, weight_out, tag_buf, sems = refs
    width = patch_ref.shape[1]
    patch_count = patch_ref.shape[0]
    visits = dest_ref.shape[0]
    pairs = (
        (dest_ref, tag_buf.at[0]),
        (block_ref, tag_buf.at[1]),
        (patch_ref, own_ref.at[:, :width]),
        (row_ref, row_out),
        (col_ref, col_out),
        (weight_ref, weight_out),
    )
    copies = [pltpu.make_async_copy(src, dst, sems.at[i]) for i, (src, dst) in enumerate(pairs)]
    for copy in copies:
        copy.start()
    copies[0].wait()
    copies[1].wait()
    tags = jnp.concatenate([tag_buf[0], tag_buf[1]], axis=0).astype(jnp.float32)
    tags = jnp.concatenate([tags, jnp.zeros((2 * visits, LANES - patch_count), jnp.float32)], axis=1)
    tags = jnp.concatenate([tags, jnp.zeros((LANES - 2 * visits, LANES), jnp.float32)], axis=0)
    own_ref[:, width:] = tags.T[:patch_count].astype(jnp.bfloat16)
    for copy in copies[2:]:
        copy.wait()


def parcel_kernel(row_ref, col_ref, maps_ref):
    kinds_local, _, rows = row_ref.shape
    for k in range(kinds_local):
        both = jnp.concatenate([row_ref[k].astype(jnp.float32), col_ref[k].astype(jnp.float32)], axis=0)
        both = jnp.concatenate([both, jnp.zeros((LANES, LANES - rows), jnp.float32)], axis=1)
        maps_ref[k * rows : (k + 1) * rows, :] = both.T[:rows].astype(jnp.bfloat16)


def picks(tags, dims, places):
    visits, group_blocks, per_exp, col_grid, band_grid, strips, exp_local, rows_axis = dims
    group, band, basis = places
    codes = visit_codes(tags, visits, group_blocks)
    lane = lax.broadcasted_iota(jnp.int32, (1, LANES), 1)
    exp_at = lane // (strips * col_grid)
    strip = lane // col_grid % strips
    block_row = band * (band_grid - 1) + strip
    dest = group * rows_axis + block_row // band_grid
    block = (basis * exp_local + exp_at) * per_exp + block_row % band_grid * col_grid + lane % col_grid
    want = jnp.where(exp_at < exp_local, dest * group_blocks + block, -1).astype(jnp.float32)
    hit = jnp.zeros((tags.shape[0], LANES), jnp.float32)
    for v in range(visits):
        hit = hit + jnp.where(codes[:, v : v + 1] == want, 1.0, 0.0)
    blocks = exp_local * strips * col_grid
    return hit.T[:blocks].astype(jnp.bfloat16)


def summed_into(out_ref, chunk_refs, before_ref, dims, width, blocks):
    places = (lax.axis_index("exp"), lax.axis_index("row"), lax.axis_index("basis"))
    tags = jnp.concatenate([ref[:, width:] for ref in chunk_refs], axis=0)
    pick = picks(tags, dims, places)
    step = 4 * LANES
    for start in range(0, width, step):
        rows = jnp.concatenate([ref[:, start : start + step] for ref in chunk_refs], axis=0)
        part = jnp.dot(pick, rows, preferred_element_type=jnp.float32)
        for t in range(step // LANES):
            at = (start // LANES + t) * blocks
            piece = part[:, t * LANES : (t + 1) * LANES]
            if before_ref is not None:
                piece = piece + before_ref[at : at + blocks, :]
            out_ref[at : at + blocks, :] = piece


def early_kernel(dims, width, block, kinds_local, *refs):
    chunks, parcels, (table_ref, other_ref) = refs[:6], refs[6:-7], refs[-7:-5]
    sums_ref, rows_ref, main_ref, edge_ref, wide_ref = refs[-5:]
    _, group_blocks, per_exp, col_grid, band_grid, strips, exp_local, _ = dims
    blocks = exp_local * strips * col_grid
    summed_into(sums_ref, chunks, None, dims, width, blocks)
    band = lax.axis_index("row")
    out_rows = 96
    kinds = kinds_local * len(parcels)
    src = lax.broadcasted_iota(jnp.int32, (LANES, 2 * LANES), 0)
    dst = lax.broadcasted_iota(jnp.int32, (LANES, 2 * LANES), 1)
    half = block // 2
    inner = dst % block
    wanted = inner % half * 2 + inner // half
    perm = jnp.where((src == wanted) & (dst < strips * block), 1.0, 0.0).astype(jnp.bfloat16)
    lane2 = lax.broadcasted_iota(jnp.int32, (out_rows, 2 * LANES), 1)
    spill = (out_rows - block) // 2
    lane_c = lax.broadcasted_iota(jnp.int32, (block, 2 * LANES), 1)
    lane_e = lax.broadcasted_iota(jnp.int32, (block, LANES), 1)
    for k in range(kinds):
        parcel = parcels[k // kinds_local]
        both = parcel[(k % kinds_local) * out_rows : (k % kinds_local + 1) * out_rows, :]
        moved = jnp.dot(both, perm, preferred_element_type=jnp.float32)
        gap = jnp.zeros((block, 2 * LANES), jnp.float32)
        total = None
        for s in range(strips):
            piece = jnp.where(lane2 // block == s, moved, 0.0)
            parts = [gap] * s + [piece] + [gap] * (strips - 1 - s)
            piece = jnp.concatenate(parts, axis=0)
            total = piece if total is None else total + piece
        first = total[spill : spill + 2 * block, : strips * block]
        second = total[spill + block : spill + 3 * block, : strips * block]
        chosen = jnp.where(band == 0, first, second).astype(jnp.bfloat16)
        rows_ref[k * 2 * block : (k + 1) * 2 * block, :] = chosen
        cols = both.astype(jnp.float32)
        cols = jnp.concatenate([cols, jnp.zeros((LANES - out_rows, LANES), jnp.float32)], axis=0)
        turned = cols.T[block:, :]
        turned = jnp.concatenate([turned, jnp.zeros_like(turned)], axis=1)
        for b in range(4):
            shift = (b * block - spill) % (2 * LANES)
            placed = pltpu.roll(turned, shift, 1)
            kept = placed
            if b == 0:
                kept = jnp.where(lane_c < 2 * LANES - spill, placed, 0.0)
                edge = jnp.where(lane_e >= LANES - spill, placed[:, LANES:], 0.0)
                edge_ref[0, k * LANES : k * LANES + block, :] = edge.astype(jnp.bfloat16)
                edge_ref[0, k * LANES + block : (k + 1) * LANES, :] = jnp.zeros((block, LANES), jnp.bfloat16)
            if b == 3:
                kept = jnp.where(lane_c >= spill, placed, 0.0)
                edge = jnp.where(lane_e < spill, placed[:, :LANES], 0.0)
                edge_ref[1, k * LANES + block : (k + 1) * LANES, :] = edge.astype(jnp.bfloat16)
                edge_ref[1, k * LANES : k * LANES + block, :] = jnp.zeros((block, LANES), jnp.bfloat16)
            at = k * 4 * block + b * block
            main_ref[at : at + block, :] = kept.astype(jnp.bfloat16)
    pair = (table_ref[...], other_ref[...])
    table = jnp.concatenate(
        [jnp.where(band == 0, pair[0], pair[1]), jnp.where(band == 0, pair[1], pair[0])], axis=1
    )
    src = lax.broadcasted_iota(jnp.int32, (table.shape[1], col_grid * block), 0)
    dst = lax.broadcasted_iota(jnp.int32, (table.shape[1], col_grid * block), 1)
    ahead = src - dst // block
    first_exp = lax.axis_index("basis") * exp_local
    exp_group = group_blocks // per_exp
    for x in range(exp_local):
        for s in range(strips):
            block_row = band * (band_grid - 1) + s
            line = (block_row // band_grid * exp_group + first_exp + x) * band_grid + block_row % band_grid
            spread = jnp.where(ahead == line * col_grid, 1.0, 0.0).astype(jnp.bfloat16)
            lines = jnp.dot(table, spread, preferred_element_type=jnp.float32)
            for k in range(kinds):
                wide = jnp.broadcast_to(lines[k : k + 1], (16, col_grid * block))
                at = ((x * kinds + k) * strips + s) * 16
                wide_ref[at : at + 16, :] = wide.astype(jnp.bfloat16)


def late_kernel(dims, width, block, kinds, *refs):
    chunks = refs[:6]
    (before_ref, rows_ref, main_ref, edge_ref, wide_ref, obs_ref, inv_ref, out_ref) = refs[6:14]
    sums_ref, image_ref, mid_ref, side_ref = refs[14:]
    _, _, _, col_grid, band_grid, strips, exp_local, _ = dims
    blocks = exp_local * strips * col_grid
    summed_into(sums_ref, chunks, before_ref, dims, width, blocks)
    half = block // 2
    low = lax.broadcasted_iota(jnp.int32, (half, LANES), 1) < block
    tall = strips * block
    wide_cols = col_grid * block
    band_rows = band_grid * block
    for x in range(exp_local):
        for s in range(strips):
            for m in range(col_grid // 2):
                n = (x * strips + s) * col_grid + 2 * m
                a = sums_ref[pl.ds(n, half, stride=blocks), :]
                b = sums_ref[pl.ds(n + 1, half, stride=blocks), :]
                even = jnp.where(low, a, pltpu.roll(b, block, 1))
                odd = jnp.where(low, pltpu.roll(a, block, 1), b)
                at = s * block
                cols = slice(m * LANES, (m + 1) * LANES)
                image_ref[x, at : at + half, cols] = even.astype(jnp.bfloat16)
                image_ref[x, at + half : at + block, cols] = odd.astype(jnp.bfloat16)
    window = 4 * block
    for x in range(exp_local):
        for k in range(kinds):
            image = image_ref[x].reshape(strips, block // 16, 16, wide_cols)
            at = (x * kinds + k) * strips * 16
            wide = wide_ref[at : at + strips * 16, :].reshape(strips, 1, 16, wide_cols)
            scaled = (image * wide).reshape(tall, wide_cols)
            rows = rows_ref[k * band_rows : (k + 1) * band_rows, :]
            mid = jnp.dot(rows, scaled, preferred_element_type=jnp.float32).astype(jnp.bfloat16)
            for w in range(2):
                top = (w * exp_local + x) * band_rows
                mid_ref[top : top + band_rows, k * window : (k + 1) * window] = mid[:, w * window : (w + 1) * window]
            at = x * band_rows
            cols = slice(k * LANES, (k + 1) * LANES)
            side_ref[0, at : at + band_rows, cols] = mid[:, window : window + LANES]
            side_ref[1, at : at + band_rows, cols] = mid[:, window - LANES : window]
    tall2 = exp_local * band_rows
    for w in range(2):
        main = jnp.dot(mid_ref[w * tall2 : (w + 1) * tall2, :], main_ref[...], preferred_element_type=jnp.float32)
        side = jnp.dot(side_ref[w], edge_ref[w], preferred_element_type=jnp.float32)
        for x in range(exp_local):
            rows = slice(x * band_rows, (x + 1) * band_rows)
            noise = jnp.sqrt(jnp.full((1, LANES), inv_ref[x], jnp.float32))
            for t in range(2):
                model = main[rows, t * LANES : (t + 1) * LANES]
                if t == 1 - w:
                    model = model + side[rows]
                cols = slice(w * window + t * LANES, w * window + (t + 1) * LANES)
                out_ref[x, :, cols] = noise * (obs_ref[x, :, cols].astype(jnp.float32) - model)


def gathered_device(
    scene_patches, visit_dest, visit_block, row_maps, col_maps, psf_weights, inv_variance, observed
):
    n_exp, n_row, n_basis = (lax.axis_size(a) for a in ("exp", "row", "basis"))
    patch_count, visits = visit_dest.shape
    width = scene_patches.shape[1]
    exp_local, band_rows, tile_cols = observed.shape
    exp_group, kinds_local, band_grid, col_grid = psf_weights.shape
    block = row_maps.shape[2]
    out_width = row_maps.shape[1]
    strips = band_grid + 1
    per_exp = band_grid * col_grid
    group_blocks = exp_group * per_exp
    kinds = kinds_local * n_basis
    basis = lax.axis_index("basis")
    dims = (visits, group_blocks, per_exp, col_grid, band_grid, strips, exp_local, n_row)
    blocks = exp_local * strips * col_grid

    f32, bf16 = jnp.float32, jnp.bfloat16
    params = pltpu.CompilerParams(vmem_limit_bytes=VMEM_BYTES)
    packed = (
        scene_patches,
        visit_dest.T,
        visit_block.T,
        jnp.swapaxes(row_maps, 1, 2),
        jnp.swapaxes(col_maps, 1, 2),
        psf_weights,
    )
    own, row_now, col_now, weights_now = pl.pallas_call(
        pack_kernel,
        out_shape=[
            jax.ShapeDtypeStruct((patch_count, width + LANES), bf16),
            jax.ShapeDtypeStruct((kinds_local, block, out_width), bf16),
            jax.ShapeDtypeStruct((kinds_local, block, out_width), bf16),
            jax.ShapeDtypeStruct(psf_weights.shape, bf16),
        ],
        in_specs=[pl.BlockSpec(memory_space=pltpu.HBM)] * 6,
        out_specs=in_vmem(4),
        scratch_shapes=[pltpu.VMEM((2, visits, patch_count), jnp.int32), pltpu.SemaphoreType.DMA((6,))],
        compiler_params=params,
    )(*(pltpu.with_memory_space_constraint(v, pltpu.HBM) for v in packed))
    part = patch_count // n_basis
    own_part = lax.dynamic_slice_in_dim(own, basis * part, part, 0)
    far = []
    for s in range(n_exp - 1, 1, -1):
        far.append(swapped(own_part, "exp", s))
    near = swapped(own, "exp", 1)
    maps = pl.pallas_call(
        parcel_kernel,
        out_shape=jax.ShapeDtypeStruct((kinds_local * out_width, LANES), bf16),
        in_specs=in_vmem(2),
        out_specs=in_vmem(1)[0],
        compiler_params=params,
    )(row_now, col_now)
    table = jnp.swapaxes(weights_now, 0, 1).reshape(kinds_local, -1)
    table = jnp.pad(table, ((0, 16 - kinds_local), (0, 0)))
    maps = jnp.concatenate([maps, table], axis=0)
    parcels = [maps]
    for s in range(1, n_basis):
        parcels.append(swapped(maps, "basis", s))
    own_other = swapped(own, "row", 1)
    far = jnp.concatenate(far, axis=0)
    spread = []
    for s in range(n_basis - 1, 0, -1):
        spread.append(swapped(far, "basis", s))
    near_other = swapped(near, "row", 1)
    far_other = swapped(far, "row", 1)
    table = jnp.concatenate(
        [p[kinds_local * out_width : kinds_local * out_width + kinds_local] for p in parcels], axis=0
    )
    table_other = swapped(table, "row", 1)
    spread_other = []
    for s, v in zip(range(n_basis - 1, 0, -1), spread):
        spread_other.append(swapped(v, "row", 1))

    early = [own, near, far, own_other, near_other, far_other] + parcels + [table, table_other]
    shapes = [
        jax.ShapeDtypeStruct((width // LANES * blocks, LANES), f32),
        jax.ShapeDtypeStruct((kinds * band_rows, strips * block), bf16),
        jax.ShapeDtypeStruct((kinds * 4 * block, 4 * block), bf16),
        jax.ShapeDtypeStruct((2, kinds * LANES, LANES), bf16),
        jax.ShapeDtypeStruct((exp_local * kinds * strips * 16, tile_cols), bf16),
    ]
    early_call = pl.pallas_call(
        functools.partial(early_kernel, dims, width, block, kinds_local),
        out_shape=shapes,
        in_specs=in_vmem(len(early)),
        out_specs=in_vmem(len(shapes)),
        compiler_params=params,
    )
    prepared = early_call(*early)
    late = spread + spread_other + list(prepared) + [observed]
    return pl.pallas_call(
        functools.partial(late_kernel, dims, width, block, kinds),
        out_shape=jax.ShapeDtypeStruct(observed.shape, f32),
        in_specs=in_vmem(len(late)) + [pl.BlockSpec(memory_space=pltpu.SMEM)],
        out_specs=pl.BlockSpec(memory_space=pltpu.VMEM),
        scratch_shapes=[
            pltpu.VMEM((width // LANES * blocks, LANES), f32),
            pltpu.VMEM((exp_local, strips * block, tile_cols), bf16),
            pltpu.VMEM((2 * exp_local * band_rows, kinds * 4 * block), bf16),
            pltpu.VMEM((2, exp_local * band_rows, kinds * LANES), bf16),
        ],
        compiler_params=params,
    )(*late, inv_variance)


def passed_along(value, axis, by):
    length = lax.axis_size(axis)
    pairs = [(i, i + by) for i in range(length) if 0 <= i + by < length]
    return lax.ppermute(value, axis, pairs)


def pad_last(values, lower, upper):
    widths = [(0, 0)] * (values.ndim - 1) + [(lower, upper)]
    return jnp.pad(values, widths)


def fold_last(values, block_size):
    blocks_along = values.shape[-2]
    edge_width = values.shape[-1] - block_size
    lead = values.shape[:-2]
    head_part = values[..., :block_size].reshape(lead + (blocks_along * block_size,))
    tail_part = pad_last(values[..., block_size:], 0, block_size - edge_width)
    tail_part = tail_part.reshape(lead + (blocks_along * block_size,))
    head_part = pad_last(head_part, 0, edge_width)
    tail_part = pad_last(tail_part, block_size, 0)[..., : blocks_along * block_size + edge_width]
    return head_part + tail_part


def fold_blocks(images, block_size):
    images = jnp.swapaxes(images, -3, -2)
    images = fold_last(images, block_size)
    images = jnp.moveaxis(images, -1, -3)
    images = fold_last(images, block_size)
    return jnp.swapaxes(images, -1, -2)


def band_model(block_rows, weights, row_ops, col_ops, spill_rows, tile_cols):
    count_exp, kind_count, block_grid, col_grid = weights.shape
    block_size = row_ops.shape[2]
    out_width = row_ops.shape[1]
    tile_blocks = block_rows.reshape(-1, block_size, block_size)
    smeared = jnp.einsum(
        "nij,kcj->knic", tile_blocks, col_ops, preferred_element_type=jnp.float32
    ).astype(jnp.bfloat16)
    smeared = lax.optimization_barrier(smeared)
    scales = jnp.swapaxes(weights, 0, 1).reshape(kind_count, -1).astype(jnp.float32)
    scaled = (scales[:, :, None, None] * smeared).astype(jnp.bfloat16)
    images = jnp.einsum("kor,knrc->noc", row_ops, scaled, preferred_element_type=jnp.float32)
    images = images.reshape(count_exp, block_grid, col_grid, out_width, out_width)
    canvas = fold_blocks(images, block_size)
    return canvas[:, :, spill_rows : spill_rows + tile_cols]


def exchanged_device(
    scene_patches, visit_dest, visit_block, row_maps, col_maps, psf_weights, inv_variance, observed
):
    group_size = lax.axis_size("exp") * lax.axis_size("row")
    patch_count, visit_count = visit_dest.shape
    capacity = max(2, 2 * patch_count * visit_count // group_size)
    exp_local, band_rows, tile_cols = observed.shape
    _, _, block_grid, col_grid = psf_weights.shape
    block_size = row_maps.shape[2]
    spill_rows = (row_maps.shape[1] - block_size) // 2
    per_exposure = block_grid * col_grid
    flat_dest = visit_dest.reshape(-1)
    matches = (flat_dest[:, None] == jnp.arange(group_size, dtype=jnp.int32)[None, :]).astype(
        jnp.int32
    )
    slot_rank = jnp.sum(jnp.cumsum(matches, axis=0) * matches, axis=1) - 1
    slot_index = flat_dest * capacity + slot_rank
    select_mat = (
        slot_index[None, :] == jnp.arange(group_size * capacity, dtype=jnp.int32)[:, None]
    ).astype(jnp.int32)
    tagged = jnp.sum(select_mat * (visit_block.reshape(-1) + 1)[None, :], axis=1).astype(
        jnp.bfloat16
    )
    picker = jnp.sum(
        select_mat.reshape(group_size * capacity, patch_count, visit_count), axis=2
    ).astype(jnp.bfloat16)
    outgoing = jnp.dot(picker, scene_patches, preferred_element_type=jnp.float32).astype(
        jnp.bfloat16
    )
    shaped = outgoing.reshape(group_size, capacity, -1)
    labels = tagged.reshape(group_size, capacity)
    arrived, arrived_tags = (
        lax.all_to_all(shaped, ("exp", "row"), split_axis=0, concat_axis=0, tiled=True),
        lax.all_to_all(labels, ("exp", "row"), split_axis=0, concat_axis=0, tiled=True),
    )
    arrived = arrived.reshape(group_size * capacity, -1)
    arrived_tags = arrived_tags.reshape(-1).astype(jnp.int32)
    row_all, col_all, weight_all = (
        lax.all_gather(row_maps, "basis", axis=0, tiled=True),
        lax.all_gather(col_maps, "basis", axis=0, tiled=True),
        lax.all_gather(psf_weights, "basis", axis=1, tiled=True),
    )
    first_exp = lax.axis_index("basis") * exp_local
    wanted = first_exp * per_exposure + 1 + jnp.arange(exp_local * per_exposure, dtype=jnp.int32)
    placing = (arrived_tags[None, :] == wanted[:, None]).astype(jnp.bfloat16)
    own_blocks = jnp.dot(placing, arrived, preferred_element_type=jnp.float32).astype(jnp.bfloat16)
    own_weights = lax.dynamic_slice_in_dim(weight_all, first_exp, exp_local, 0)
    model_band = band_model(own_blocks, own_weights, row_all, col_all, spill_rows, tile_cols)
    upper_spill = model_band[:, :spill_rows]
    lower_spill = model_band[:, spill_rows + band_rows :]
    from_above = passed_along(lower_spill.astype(jnp.bfloat16), "row", 1).astype(lower_spill.dtype)
    from_below = passed_along(upper_spill.astype(jnp.bfloat16), "row", -1).astype(upper_spill.dtype)
    core_rows = model_band[:, spill_rows : spill_rows + band_rows]
    core_rows = core_rows.at[:, :spill_rows].add(from_above)
    core_rows = core_rows.at[:, band_rows - spill_rows :].add(from_below)
    return jnp.sqrt(inv_variance)[:, None, None] * (observed.astype(jnp.float32) - core_rows)


def gathers(mesh, patch_count, visits):
    n_exp, n_row, n_basis = mesh.shape["exp"], mesh.shape["row"], mesh.shape["basis"]
    capacity = max(2, 2 * patch_count * visits // (n_exp * n_row))
    powers = all(n & (n - 1) == 0 for n in (n_exp, n_basis)) and n_exp > 2 and n_basis > 2
    return capacity >= patch_count and powers and n_row == 2 and patch_count % (8 * n_basis) == 0


def in_layer(*arrays):
    return gathered_device(*arrays)


def solution(mesh):
    def step(*arrays):
        patch_total, visits = arrays[1].shape
        patch_count = patch_total // (mesh.shape["exp"] * mesh.shape["row"])
        gather = gathers(mesh, patch_count, visits)
        sharded = jax.shard_map(
            in_layer if gather else exchanged_device,
            mesh=mesh,
            in_specs=(
                P(("exp", "row"), None),
                P(("exp", "row"), None),
                P(("exp", "row"), None),
                P("basis", None, None),
                P("basis", None, None),
                P("exp", "basis", "row", None),
                P(("exp", "basis")),
                P(("exp", "basis"), "row", None),
            ),
            out_specs=P(("exp", "basis"), "row", None),
            check_vma=False,
        )
        return sharded(*arrays)

    return step
```

```python
import functools
import jax
import jax.numpy as jnp
from jax import lax
from jax.experimental import pallas as pl
from jax.experimental.pallas import tpu as pltpu
from jax.sharding import PartitionSpec as P


LANES = 128
TAGS_AT = 64
VMEM_BYTES = 28 * 1024 * 1024


def swapped(value, axis, by):
    length = lax.axis_size(axis)
    return lax.ppermute(value, axis, [(i, i ^ by) for i in range(length)])


def in_vmem(count):
    return [pl.BlockSpec(memory_space=pltpu.VMEM)] * count


def pack_kernel(patch_ref, dest_ref, block_ref, row_ref, col_ref, weight_ref, *refs):
    own_ref, row_out, col_out, weight_out, tag_buf, sems = refs
    width = patch_ref.shape[1]
    patch_count = patch_ref.shape[0]
    visits = dest_ref.shape[0]
    pairs = (
        (dest_ref, tag_buf.at[0]),
        (block_ref, tag_buf.at[1]),
        (patch_ref, own_ref.at[:, :width]),
        (row_ref, row_out),
        (col_ref, col_out),
        (weight_ref, weight_out),
    )
    copies = [pltpu.make_async_copy(src, dst, sems.at[i]) for i, (src, dst) in enumerate(pairs)]
    for copy in copies:
        copy.start()
    copies[0].wait()
    copies[1].wait()
    tags = jnp.concatenate([tag_buf[0], tag_buf[1]], axis=0).astype(jnp.float32)
    tags = jnp.concatenate([tags, jnp.zeros((2 * visits, LANES - patch_count), jnp.float32)], axis=1)
    tags = jnp.concatenate([tags, jnp.zeros((LANES - 2 * visits, LANES), jnp.float32)], axis=0)
    tags = tags.T[:patch_count]
    part = patch_count // lax.axis_size("basis")
    pieces = [tags[at : at + part] for at in range(0, patch_count, part)]
    every = pieces[0]
    for i, piece in enumerate(pieces[1:], 1):
        every = every + pltpu.roll(piece, 2 * visits * i, 1)
    tags = jnp.concatenate([every + pltpu.roll(piece, TAGS_AT, 1) for piece in pieces], axis=0)
    own_ref[:, width:] = tags.astype(jnp.bfloat16)
    for copy in copies[2:]:
        copy.wait()


def parcel_kernel(row_ref, col_ref, maps_ref):
    kinds_local, _, rows = row_ref.shape
    share = kinds_local // lax.axis_size("row")
    first = lax.axis_index("row") * share
    for i in range(share):
        both = [ref[first + i].astype(jnp.float32) for ref in (row_ref, col_ref)]
        both = jnp.concatenate(both, axis=0)
        both = jnp.concatenate([both, jnp.zeros((LANES, LANES - rows), jnp.float32)], axis=1)
        maps_ref[i * rows : (i + 1) * rows, :] = both.T[:rows].astype(jnp.bfloat16)


def stack_kernel(*refs):
    *parts, out_ref = refs
    at = 0
    for part in parts:
        out_ref[at : at + part.shape[0], :] = part[...]
        at += part.shape[0]


def picks(tags, dims):
    visits, group_blocks, per_exp, col_grid, band_grid, strips, exp_local, rows_axis = dims
    group, band, basis = lax.axis_index("exp"), lax.axis_index("row"), lax.axis_index("basis")
    codes = tags[:, :visits] * group_blocks + tags[:, visits : 2 * visits]
    lane = lax.broadcasted_iota(jnp.int32, (1, LANES), 1)
    exp_at = lane // (strips * col_grid)
    strip = lane // col_grid % strips
    block_row = band * (band_grid - 1) + strip
    dest = group * rows_axis + block_row // band_grid
    block = (basis * exp_local + exp_at) * per_exp + block_row % band_grid * col_grid + lane % col_grid
    want = jnp.where(exp_at < exp_local, dest * group_blocks + block, -1).astype(jnp.float32)
    hit = jnp.zeros((tags.shape[0], LANES), jnp.float32)
    for v in range(visits):
        hit = hit + jnp.where(codes[:, v : v + 1] == want, 1.0, 0.0)
    return hit.T[: exp_local * strips * col_grid].astype(jnp.bfloat16)


def tags_of(ref, width, lane):
    return pltpu.roll(ref[:, width:].astype(jnp.float32), (LANES - lane) % LANES, 1)


def pick_kernel(dims, width, sources, near_ref, near_other_ref, far_ref, far_other_ref, pick_ref):
    tags = [tags_of(ref, width, TAGS_AT) for ref in (near_ref, near_other_ref)]
    basis = lax.axis_index("basis")
    for ref in (far_ref, far_other_ref):
        tags += [tags_of(ref, width, (basis ^ s) * 2 * dims[0]) for s in range(sources - 1, 0, -1)]
    pick_ref[...] = picks(jnp.concatenate(tags, axis=0), dims)


def summed_into(out_ref, pick, chunk_refs, before_ref, width, blocks):
    step = 4 * LANES
    for start in range(0, width, step):
        rows = jnp.concatenate([ref[:, start : start + step] for ref in chunk_refs], axis=0)
        part = jnp.dot(pick, rows, preferred_element_type=jnp.float32)
        for t in range(step // LANES):
            at = (start // LANES + t) * blocks
            piece = part[:, t * LANES : (t + 1) * LANES]
            if before_ref is not None:
                piece = piece + before_ref[at : at + blocks, :]
            out_ref[at : at + blocks, :] = piece


def early_kernel(dims, width, block, kinds, sources, *refs):
    chunks, stacks = refs[:4], refs[4:6]
    sums_ref, rows_ref, main_ref, edge_ref, wide_ref = refs[-5:]
    _, group_blocks, per_exp, col_grid, band_grid, strips, exp_local, _ = dims
    blocks = exp_local * strips * col_grid
    tags = jnp.concatenate([tags_of(ref, width, TAGS_AT) for ref in chunks], axis=0)
    summed_into(sums_ref, picks(tags, dims), chunks, None, width, blocks)
    band = lax.axis_index("row")
    out_rows = 96
    share = kinds // (2 * sources)
    tall = stacks[0].shape[0] // sources
    src = lax.broadcasted_iota(jnp.int32, (LANES, 2 * LANES), 0)
    dst = lax.broadcasted_iota(jnp.int32, (LANES, 2 * LANES), 1)
    half = block // 2
    inner = dst % block
    wanted = inner % half * 2 + inner // half
    perm = jnp.where((src == wanted) & (dst < strips * block), 1.0, 0.0).astype(jnp.bfloat16)
    lane2 = lax.broadcasted_iota(jnp.int32, (out_rows, 2 * LANES), 1)
    spill = (out_rows - block) // 2
    lane_c = lax.broadcasted_iota(jnp.int32, (block, 2 * LANES), 1)
    lane_e = lax.broadcasted_iota(jnp.int32, (spill, LANES), 1)
    for k in range(kinds):
        at = k // share % sources * tall + k % share * out_rows
        both = stacks[k // (share * sources)][at : at + out_rows, :]
        moved = jnp.dot(both, perm, preferred_element_type=jnp.float32)
        gap = jnp.zeros((block, 2 * LANES), jnp.float32)
        total = None
        for s in range(strips):
            piece = jnp.where(lane2 // block == s, moved, 0.0)
            parts = [gap] * s + [piece] + [gap] * (strips - 1 - s)
            piece = jnp.concatenate(parts, axis=0)
            total = piece if total is None else total + piece
        first = total[spill : spill + 2 * block, : strips * block]
        second = total[spill + block : spill + 3 * block, : strips * block]
        chosen = jnp.where(band == 0, first, second).astype(jnp.bfloat16)
        rows_ref[k * 2 * block : (k + 1) * 2 * block, :] = chosen
        cols = both.astype(jnp.float32)
        left = jnp.where(lane_e < block, 0.0, cols[out_rows - spill :])
        right = jnp.where(lane_e < block, pltpu.roll(cols[:spill], block, 1), 0.0)
        both_edges = jnp.concatenate([left, right], axis=0)
        edge_ref[:, k * LANES : (k + 1) * LANES] = both_edges.astype(jnp.bfloat16)
        cols = jnp.concatenate([cols, jnp.zeros((LANES - out_rows, LANES), jnp.float32)], axis=0)
        turned = cols.T[block:, :]
        turned = jnp.concatenate([turned, jnp.zeros_like(turned)], axis=1)
        for b in range(4):
            shift = (b * block - spill) % (2 * LANES)
            placed = pltpu.roll(turned, shift, 1)
            kept = placed
            if b == 0:
                kept = jnp.where(lane_c < 2 * LANES - spill, placed, 0.0)
            if b == 3:
                kept = jnp.where(lane_c >= spill, placed, 0.0)
            at = k * 4 * block + b * block
            main_ref[at : at + block, :] = kept.astype(jnp.bfloat16)
    deep = tall - share * out_rows
    row = lax.broadcasted_iota(jnp.int32, (kinds, sources * deep), 0)
    col = lax.broadcasted_iota(jnp.int32, (kinds, sources * deep), 1)
    core = jnp.where(row < share * sources, band, 1 - band)
    wanted = row // share % sources * deep + core * share + row % share
    find = jnp.where(col == wanted, 1.0, 0.0).astype(jnp.bfloat16)
    pair = []
    for stack in stacks:
        lines = [stack[(s + 1) * tall - deep : (s + 1) * tall, :] for s in range(sources)]
        lines = jnp.concatenate(lines, axis=0)
        pair.append(jnp.dot(find, lines, preferred_element_type=jnp.float32))
    table = [jnp.where(band == b, pair[0], pair[1]).astype(jnp.bfloat16) for b in range(2)]
    table = jnp.concatenate(table, axis=1)
    src = lax.broadcasted_iota(jnp.int32, (table.shape[1], col_grid * block), 0)
    dst = lax.broadcasted_iota(jnp.int32, (table.shape[1], col_grid * block), 1)
    ahead = src - dst // block
    first_exp = lax.axis_index("basis") * exp_local
    exp_group = group_blocks // per_exp
    for x in range(exp_local):
        for s in range(strips):
            block_row = band * (band_grid - 1) + s
            line = (block_row // band_grid * exp_group + first_exp + x) * band_grid + block_row % band_grid
            spread = jnp.where(ahead == line * col_grid, 1.0, 0.0).astype(jnp.bfloat16)
            lines = jnp.dot(table, spread, preferred_element_type=jnp.float32)
            for k in range(kinds):
                wide = jnp.broadcast_to(lines[k : k + 1], (16, col_grid * block))
                at = ((x * kinds + k) * strips + s) * 16
                wide_ref[at : at + 16, :] = wide.astype(jnp.bfloat16)


def late_kernel(dims, width, block, kinds, *refs):
    chunks = refs[:-13]
    (pick_ref, before_ref, rows_ref, main_ref, edge_ref, wide_ref, obs_ref, inv_ref, out_ref) = refs[-13:-4]
    sums_ref, image_ref, mid_ref, side_ref = refs[-4:]
    _, _, _, col_grid, band_grid, strips, exp_local, _ = dims
    blocks = exp_local * strips * col_grid
    summed_into(sums_ref, pick_ref[...], chunks, before_ref, width, blocks)
    half = block // 2
    low = lax.broadcasted_iota(jnp.int32, (half, LANES), 1) < block
    tall = strips * block
    window = 4 * block
    band_rows = band_grid * block
    low_band = lax.broadcasted_iota(jnp.int32, (band_rows, LANES), 1) < block

    def laid_out(x, s, m):
        n = (x * strips + s) * col_grid + 2 * m
        a = sums_ref[pl.ds(n, half, stride=blocks), :]
        b = sums_ref[pl.ds(n + 1, half, stride=blocks), :]
        even = jnp.where(low, a, pltpu.roll(b, block, 1))
        odd = jnp.where(low, pltpu.roll(a, block, 1), b)
        at = s * block
        cols = slice(m * LANES, (m + 1) * LANES)
        image_ref[x, at : at + half, cols] = even.astype(jnp.bfloat16)
        image_ref[x, at + half : at + block, cols] = odd.astype(jnp.bfloat16)

    places = [[(x, s, m) for s in range(strips) for m in range(col_grid // 2)] for x in range(exp_local)]
    for place in places[0]:
        laid_out(*place)
    for x in range(exp_local):
        ahead = places[x + 1] if x + 1 < exp_local else []
        for k in range(kinds):
            at = (x * kinds + k) * strips * 16
            rows = rows_ref[k * band_rows : (k + 1) * band_rows, :]
            mids = []
            for w in range(2):
                cols = slice(w * window, (w + 1) * window)
                image = image_ref[x, :, cols].reshape(strips, block // 16, 16, window)
                wide = wide_ref[at : at + strips * 16, cols].reshape(strips, 1, 16, window)
                scaled = (image * wide).reshape(tall, window)
                mid = jnp.dot(rows, scaled, preferred_element_type=jnp.float32)
                top = (w * exp_local + x) * band_rows
                mid_ref[top : top + band_rows, k * window : (k + 1) * window] = mid.astype(jnp.bfloat16)
                mids.append(mid[:, :LANES] if w else mid[:, window - LANES :])
            side = jnp.where(low_band, mids[1], mids[0])
            side_ref[x * band_rows : (x + 1) * band_rows, k * LANES : (k + 1) * LANES] = side.astype(jnp.bfloat16)
            for place in ahead[k :: kinds]:
                laid_out(*place)
    tall2 = exp_local * band_rows
    spill = edge_ref.shape[0] // 2
    side = lax.dot_general(
        edge_ref[...], side_ref[...], (((1,), (1,)), ((), ())), preferred_element_type=jnp.float32
    )
    gap = jnp.zeros((LANES - 2 * spill, tall2), jnp.float32)
    side = jnp.concatenate([side[:spill], gap, side[spill:]], axis=0).T
    low_all = lax.broadcasted_iota(jnp.int32, (tall2, LANES), 1) < block
    for w in range(2):
        main = jnp.dot(mid_ref[w * tall2 : (w + 1) * tall2, :], main_ref[...], preferred_element_type=jnp.float32)
        edge = jnp.where(low_all, side, 0.0) if w else jnp.where(low_all, 0.0, side)
        for x in range(exp_local):
            rows = slice(x * band_rows, (x + 1) * band_rows)
            noise = jnp.sqrt(jnp.full((1, LANES), inv_ref[x], jnp.float32))
            for t in range(2):
                model = main[rows, t * LANES : (t + 1) * LANES]
                if t == 1 - w:
                    model = model + edge[rows]
                cols = slice(w * window + t * LANES, w * window + (t + 1) * LANES)
                out_ref[x, :, cols] = noise * (obs_ref[x, :, cols].astype(jnp.float32) - model)


def gathered_device(
    scene_patches, visit_dest, visit_block, row_maps, col_maps, psf_weights, inv_variance, observed
):
    n_exp, n_row, n_basis = (lax.axis_size(a) for a in ("exp", "row", "basis"))
    patch_count, visits = visit_dest.shape
    width = scene_patches.shape[1]
    exp_local, band_rows, tile_cols = observed.shape
    exp_group, kinds_local, band_grid, col_grid = psf_weights.shape
    block = row_maps.shape[2]
    out_width = row_maps.shape[1]
    strips = band_grid + 1
    per_exp = band_grid * col_grid
    group_blocks = exp_group * per_exp
    kinds = kinds_local * n_basis
    basis = lax.axis_index("basis")
    dims = (visits, group_blocks, per_exp, col_grid, band_grid, strips, exp_local, n_row)
    blocks = exp_local * strips * col_grid
    spill = (out_width - block) // 2

    f32, bf16 = jnp.float32, jnp.bfloat16
    params = pltpu.CompilerParams(vmem_limit_bytes=VMEM_BYTES)
    packed = (
        scene_patches,
        visit_dest.T,
        visit_block.T,
        jnp.swapaxes(row_maps, 1, 2),
        jnp.swapaxes(col_maps, 1, 2),
        psf_weights,
    )
    own, row_now, col_now, weights_now = pl.pallas_call(
        pack_kernel,
        out_shape=[
            jax.ShapeDtypeStruct((patch_count, width + LANES), bf16),
            jax.ShapeDtypeStruct((kinds_local, block, out_width), bf16),
            jax.ShapeDtypeStruct((kinds_local, block, out_width), bf16),
            jax.ShapeDtypeStruct(psf_weights.shape, bf16),
        ],
        in_specs=[pl.BlockSpec(memory_space=pltpu.HBM)] * 6,
        out_specs=in_vmem(4),
        scratch_shapes=[pltpu.VMEM((2, visits, patch_count), jnp.int32), pltpu.SemaphoreType.DMA((6,))],
        compiler_params=params,
    )(*(pltpu.with_memory_space_constraint(v, pltpu.HBM) for v in packed))
    part = patch_count // n_basis
    own_part = lax.dynamic_slice_in_dim(own, basis * part, part, 0)
    far = []
    for s in range(n_exp - 1, 1, -1):
        far.append(swapped(own_part, "exp", s))
    maps = pl.pallas_call(
        parcel_kernel,
        out_shape=jax.ShapeDtypeStruct((kinds_local // n_row * out_width, LANES), bf16),
        in_specs=in_vmem(2),
        out_specs=in_vmem(1)[0],
        compiler_params=params,
    )(row_now, col_now)
    table = jnp.swapaxes(weights_now, 0, 1).reshape(kinds_local, -1)
    table = jnp.pad(table, ((0, 16 - kinds_local), (0, 0)))
    maps = jnp.concatenate([maps, table], axis=0)
    parcels = [maps]
    for s in range(1, n_basis):
        parcels.append(swapped(maps, "basis", s))
    near = swapped(own, "exp", 1)
    far = jnp.concatenate(far, axis=0)
    spread = []
    for s in range(n_basis - 1, 0, -1):
        spread.append(swapped(far, "basis", s))
    own_other = swapped(own, "row", 1)
    far_other = swapped(far, "row", 1)
    stack = pl.pallas_call(
        stack_kernel,
        out_shape=jax.ShapeDtypeStruct((n_basis * maps.shape[0], LANES), bf16),
        in_specs=in_vmem(n_basis),
        out_specs=in_vmem(1)[0],
        compiler_params=params,
    )(*parcels)
    stack_other = swapped(stack, "row", 1)
    near_other = swapped(near, "row", 1)
    spread_other = []
    for s, v in zip(range(n_basis - 1, 0, -1), spread):
        spread_other.append(swapped(v, "row", 1))

    early = [own, far, own_other, far_other, stack, stack_other]
    shapes = [
        jax.ShapeDtypeStruct((width // LANES * blocks, LANES), f32),
        jax.ShapeDtypeStruct((kinds * band_rows, strips * block), bf16),
        jax.ShapeDtypeStruct((kinds * 4 * block, 4 * block), bf16),
        jax.ShapeDtypeStruct((2 * spill, kinds * LANES), bf16),
        jax.ShapeDtypeStruct((exp_local * kinds * strips * 16, tile_cols), bf16),
    ]
    early_call = pl.pallas_call(
        functools.partial(early_kernel, dims, width, block, kinds, n_basis),
        out_shape=shapes,
        in_specs=in_vmem(len(early)),
        out_specs=in_vmem(len(shapes)),
        compiler_params=params,
    )
    prepared = early_call(*early)
    late_count = 2 * (patch_count + (n_basis - 1) * far.shape[0])
    pick = pl.pallas_call(
        functools.partial(pick_kernel, dims, width, n_basis),
        out_shape=jax.ShapeDtypeStruct((blocks, late_count), bf16),
        in_specs=in_vmem(4),
        out_specs=in_vmem(1)[0],
        compiler_params=params,
    )(near, near_other, far, far_other)
    late = [near, near_other] + spread + spread_other + [pick] + list(prepared) + [observed]
    return pl.pallas_call(
        functools.partial(late_kernel, dims, width, block, kinds),
        out_shape=jax.ShapeDtypeStruct(observed.shape, f32),
        in_specs=in_vmem(len(late)) + [pl.BlockSpec(memory_space=pltpu.SMEM)],
        out_specs=pl.BlockSpec(memory_space=pltpu.VMEM),
        scratch_shapes=[
            pltpu.VMEM((width // LANES * blocks, LANES), f32),
            pltpu.VMEM((exp_local, strips * block, tile_cols), bf16),
            pltpu.VMEM((2 * exp_local * band_rows, kinds * 4 * block), bf16),
            pltpu.VMEM((exp_local * band_rows, kinds * LANES), bf16),
        ],
        compiler_params=params,
    )(*late, inv_variance)


def passed_along(value, axis, by):
    length = lax.axis_size(axis)
    pairs = [(i, i + by) for i in range(length) if 0 <= i + by < length]
    return lax.ppermute(value, axis, pairs)


def pad_last(values, lower, upper):
    widths = [(0, 0)] * (values.ndim - 1) + [(lower, upper)]
    return jnp.pad(values, widths)


def fold_last(values, block_size):
    blocks_along = values.shape[-2]
    edge_width = values.shape[-1] - block_size
    lead = values.shape[:-2]
    head_part = values[..., :block_size].reshape(lead + (blocks_along * block_size,))
    tail_part = pad_last(values[..., block_size:], 0, block_size - edge_width)
    tail_part = tail_part.reshape(lead + (blocks_along * block_size,))
    head_part = pad_last(head_part, 0, edge_width)
    tail_part = pad_last(tail_part, block_size, 0)[..., : blocks_along * block_size + edge_width]
    return head_part + tail_part


def fold_blocks(images, block_size):
    images = jnp.swapaxes(images, -3, -2)
    images = fold_last(images, block_size)
    images = jnp.moveaxis(images, -1, -3)
    images = fold_last(images, block_size)
    return jnp.swapaxes(images, -1, -2)


def band_model(block_rows, weights, row_ops, col_ops, spill_rows, tile_cols):
    count_exp, kind_count, block_grid, col_grid = weights.shape
    block_size = row_ops.shape[2]
    out_width = row_ops.shape[1]
    tile_blocks = block_rows.reshape(-1, block_size, block_size)
    smeared = jnp.einsum(
        "nij,kcj->knic", tile_blocks, col_ops, preferred_element_type=jnp.float32
    ).astype(jnp.bfloat16)
    smeared = lax.optimization_barrier(smeared)
    scales = jnp.swapaxes(weights, 0, 1).reshape(kind_count, -1).astype(jnp.float32)
    scaled = (scales[:, :, None, None] * smeared).astype(jnp.bfloat16)
    images = jnp.einsum("kor,knrc->noc", row_ops, scaled, preferred_element_type=jnp.float32)
    images = images.reshape(count_exp, block_grid, col_grid, out_width, out_width)
    canvas = fold_blocks(images, block_size)
    return canvas[:, :, spill_rows : spill_rows + tile_cols]


def exchanged_device(
    scene_patches, visit_dest, visit_block, row_maps, col_maps, psf_weights, inv_variance, observed
):
    group_size = lax.axis_size("exp") * lax.axis_size("row")
    patch_count, visit_count = visit_dest.shape
    capacity = max(2, 2 * patch_count * visit_count // group_size)
    exp_local, band_rows, tile_cols = observed.shape
    _, _, block_grid, col_grid = psf_weights.shape
    block_size = row_maps.shape[2]
    spill_rows = (row_maps.shape[1] - block_size) // 2
    per_exposure = block_grid * col_grid
    flat_dest = visit_dest.reshape(-1)
    matches = (flat_dest[:, None] == jnp.arange(group_size, dtype=jnp.int32)[None, :]).astype(
        jnp.int32
    )
    slot_rank = jnp.sum(jnp.cumsum(matches, axis=0) * matches, axis=1) - 1
    slot_index = flat_dest * capacity + slot_rank
    select_mat = (
        slot_index[None, :] == jnp.arange(group_size * capacity, dtype=jnp.int32)[:, None]
    ).astype(jnp.int32)
    tagged = jnp.sum(select_mat * (visit_block.reshape(-1) + 1)[None, :], axis=1).astype(
        jnp.bfloat16
    )
    picker = jnp.sum(
        select_mat.reshape(group_size * capacity, patch_count, visit_count), axis=2
    ).astype(jnp.bfloat16)
    outgoing = jnp.dot(picker, scene_patches, preferred_element_type=jnp.float32).astype(
        jnp.bfloat16
    )
    shaped = outgoing.reshape(group_size, capacity, -1)
    labels = tagged.reshape(group_size, capacity)
    arrived, arrived_tags = (
        lax.all_to_all(shaped, ("exp", "row"), split_axis=0, concat_axis=0, tiled=True),
        lax.all_to_all(labels, ("exp", "row"), split_axis=0, concat_axis=0, tiled=True),
    )
    arrived = arrived.reshape(group_size * capacity, -1)
    arrived_tags = arrived_tags.reshape(-1).astype(jnp.int32)
    row_all, col_all, weight_all = (
        lax.all_gather(row_maps, "basis", axis=0, tiled=True),
        lax.all_gather(col_maps, "basis", axis=0, tiled=True),
        lax.all_gather(psf_weights, "basis", axis=1, tiled=True),
    )
    first_exp = lax.axis_index("basis") * exp_local
    wanted = first_exp * per_exposure + 1 + jnp.arange(exp_local * per_exposure, dtype=jnp.int32)
    placing = (arrived_tags[None, :] == wanted[:, None]).astype(jnp.bfloat16)
    own_blocks = jnp.dot(placing, arrived, preferred_element_type=jnp.float32).astype(jnp.bfloat16)
    own_weights = lax.dynamic_slice_in_dim(weight_all, first_exp, exp_local, 0)
    model_band = band_model(own_blocks, own_weights, row_all, col_all, spill_rows, tile_cols)
    upper_spill = model_band[:, :spill_rows]
    lower_spill = model_band[:, spill_rows + band_rows :]
    from_above = passed_along(lower_spill.astype(jnp.bfloat16), "row", 1).astype(lower_spill.dtype)
    from_below = passed_along(upper_spill.astype(jnp.bfloat16), "row", -1).astype(upper_spill.dtype)
    core_rows = model_band[:, spill_rows : spill_rows + band_rows]
    core_rows = core_rows.at[:, :spill_rows].add(from_above)
    core_rows = core_rows.at[:, band_rows - spill_rows :].add(from_below)
    return jnp.sqrt(inv_variance)[:, None, None] * (observed.astype(jnp.float32) - core_rows)


def gathers(mesh, patch_count, visits):
    n_exp, n_row, n_basis = mesh.shape["exp"], mesh.shape["row"], mesh.shape["basis"]
    capacity = max(2, 2 * patch_count * visits // (n_exp * n_row))
    powers = all(n & (n - 1) == 0 for n in (n_exp, n_basis)) and n_exp > 2 and n_basis > 2
    return capacity >= patch_count and powers and n_row == 2 and patch_count % (8 * n_basis) == 0


def in_layer(*arrays):
    return gathered_device(*arrays)


def solution(mesh):
    def step(*arrays):
        patch_total, visits = arrays[1].shape
        patch_count = patch_total // (mesh.shape["exp"] * mesh.shape["row"])
        gather = gathers(mesh, patch_count, visits)
        sharded = jax.shard_map(
            in_layer if gather else exchanged_device,
            mesh=mesh,
            in_specs=(
                P(("exp", "row"), None),
                P(("exp", "row"), None),
                P(("exp", "row"), None),
                P("basis", None, None),
                P("basis", None, None),
                P("exp", "basis", "row", None),
                P(("exp", "basis")),
                P(("exp", "basis"), "row", None),
            ),
            out_specs=P(("exp", "basis"), "row", None),
            check_vma=False,
        )
        return sharded(*arrays)

    return step
```

```python
import functools
import jax
import jax.numpy as jnp
from jax import lax
from jax.experimental import pallas as pl
from jax.experimental.pallas import tpu as pltpu
from jax.sharding import PartitionSpec as P


LANES = 128
TAGS_AT = 64
ROW_PAD = 4
VMEM_BYTES = 28 * 1024 * 1024


def swapped(value, axis, by):
    length = lax.axis_size(axis)
    return lax.ppermute(value, axis, [(i, i ^ by) for i in range(length)])


def in_vmem(count):
    return [pl.BlockSpec(memory_space=pltpu.VMEM)] * count


def pack_kernel(patch_ref, dest_ref, block_ref, row_ref, col_ref, weight_ref, *refs):
    own_ref, row_out, col_out, weight_out, tag_buf, sems = refs
    width = patch_ref.shape[1]
    patch_count = patch_ref.shape[0]
    visits = dest_ref.shape[0]
    pairs = (
        (dest_ref, tag_buf.at[0]),
        (block_ref, tag_buf.at[1]),
        (patch_ref, own_ref.at[:, :width]),
        (row_ref, row_out),
        (col_ref, col_out),
        (weight_ref, weight_out),
    )
    copies = [pltpu.make_async_copy(src, dst, sems.at[i]) for i, (src, dst) in enumerate(pairs)]
    for copy in copies:
        copy.start()
    copies[0].wait()
    copies[1].wait()
    tags = jnp.concatenate([tag_buf[0], tag_buf[1]], axis=0).astype(jnp.float32)
    tags = jnp.concatenate([tags, jnp.zeros((2 * visits, LANES - patch_count), jnp.float32)], axis=1)
    tags = jnp.concatenate([tags, jnp.zeros((LANES - 2 * visits, LANES), jnp.float32)], axis=0)
    tags = tags.T[:patch_count]
    part = patch_count // lax.axis_size("basis")
    pieces = [tags[at : at + part] for at in range(0, patch_count, part)]
    every = pieces[0]
    for i, piece in enumerate(pieces[1:], 1):
        every = every + pltpu.roll(piece, 2 * visits * i, 1)
    tags = jnp.concatenate([every + pltpu.roll(piece, TAGS_AT, 1) for piece in pieces], axis=0)
    own_ref[:, width:] = tags.astype(jnp.bfloat16)
    for copy in copies[2:]:
        copy.wait()


def parcel_kernel(row_ref, col_ref, maps_ref):
    kinds_local, _, rows = row_ref.shape
    share = kinds_local // lax.axis_size("row")
    first = lax.axis_index("row") * share
    for i in range(share):
        both = [ref[first + i].astype(jnp.float32) for ref in (row_ref, col_ref)]
        both = jnp.concatenate(both, axis=0)
        both = jnp.concatenate([both, jnp.zeros((LANES, LANES - rows), jnp.float32)], axis=1)
        maps_ref[i * rows : (i + 1) * rows, :] = both.T[:rows].astype(jnp.bfloat16)


def stack_kernel(*refs):
    *parts, out_ref = refs
    at = 0
    for part in parts:
        out_ref[at : at + part.shape[0], :] = part[...]
        at += part.shape[0]


def picks(tags, dims):
    visits, group_blocks, per_exp, col_grid, band_grid, strips, exp_local, rows_axis = dims
    group, band, basis = lax.axis_index("exp"), lax.axis_index("row"), lax.axis_index("basis")
    codes = tags[:, :visits] * group_blocks + tags[:, visits : 2 * visits]
    lane = lax.broadcasted_iota(jnp.int32, (1, LANES), 1)
    exp_at = lane // (strips * col_grid)
    strip = lane // col_grid % strips
    block_row = band * (band_grid - 1) + strip
    dest = group * rows_axis + block_row // band_grid
    block = (basis * exp_local + exp_at) * per_exp + block_row % band_grid * col_grid + lane % col_grid
    want = jnp.where(exp_at < exp_local, dest * group_blocks + block, -1).astype(jnp.float32)
    hit = jnp.zeros((tags.shape[0], LANES), jnp.float32)
    for v in range(visits):
        hit = hit + jnp.where(codes[:, v : v + 1] == want, 1.0, 0.0)
    return hit.T[: exp_local * strips * col_grid].astype(jnp.bfloat16)


def tags_of(ref, width, lane):
    return pltpu.roll(ref[:, width:].astype(jnp.float32), (LANES - lane) % LANES, 1)


def pick_kernel(dims, width, sources, near_ref, near_other_ref, far_ref, far_other_ref, pick_ref):
    tags = [tags_of(ref, width, TAGS_AT) for ref in (near_ref, near_other_ref)]
    basis = lax.axis_index("basis")
    for ref in (far_ref, far_other_ref):
        tags += [tags_of(ref, width, (basis ^ s) * 2 * dims[0]) for s in range(sources - 1, 0, -1)]
    pick_ref[...] = picks(jnp.concatenate(tags, axis=0), dims)


def summed_into(out_ref, pick, chunk_refs, before_ref, width, blocks, pitch):
    step = 4 * LANES
    for start in range(0, width, step):
        rows = jnp.concatenate([ref[:, start : start + step] for ref in chunk_refs], axis=0)
        part = jnp.dot(pick, rows, preferred_element_type=jnp.float32)
        for t in range(step // LANES):
            at = (start // LANES + t) * blocks
            piece = part[:, t * LANES : (t + 1) * LANES]
            if before_ref is not None:
                piece = piece + before_ref[at : at + blocks, :]
            at = (start // LANES + t) * pitch
            out_ref[at : at + blocks, :] = piece


def early_kernel(dims, width, block, kinds, sources, *refs):
    chunks, stacks = refs[:4], refs[4:6]
    sums_ref, rows_ref, main_ref, edge_ref, wide_ref = refs[-5:]
    _, group_blocks, per_exp, col_grid, band_grid, strips, exp_local, _ = dims
    blocks = exp_local * strips * col_grid
    tags = jnp.concatenate([tags_of(ref, width, TAGS_AT) for ref in chunks], axis=0)
    summed_into(sums_ref, picks(tags, dims), chunks, None, width, blocks, blocks)
    band = lax.axis_index("row")
    out_rows = 96
    share = kinds // (2 * sources)
    tall = stacks[0].shape[0] // sources
    src = lax.broadcasted_iota(jnp.int32, (LANES, 2 * LANES), 0)
    dst = lax.broadcasted_iota(jnp.int32, (LANES, 2 * LANES), 1)
    half = block // 2
    inner = dst % block
    wanted = inner % half * 2 + inner // half
    perm = jnp.where((src == wanted) & (dst < strips * block), 1.0, 0.0).astype(jnp.bfloat16)
    lane2 = lax.broadcasted_iota(jnp.int32, (out_rows, 2 * LANES), 1)
    spill = (out_rows - block) // 2
    lane_c = lax.broadcasted_iota(jnp.int32, (block, 2 * LANES), 1)
    lane_e = lax.broadcasted_iota(jnp.int32, (spill, LANES), 1)
    for k in range(kinds):
        at = k // share % sources * tall + k % share * out_rows
        both = stacks[k // (share * sources)][at : at + out_rows, :]
        moved = jnp.dot(both, perm, preferred_element_type=jnp.float32)
        gap = jnp.zeros((block, 2 * LANES), jnp.float32)
        total = None
        for s in range(strips):
            piece = jnp.where(lane2 // block == s, moved, 0.0)
            parts = [gap] * s + [piece] + [gap] * (strips - 1 - s)
            piece = jnp.concatenate(parts, axis=0)
            total = piece if total is None else total + piece
        first = total[spill : spill + 2 * block, : strips * block]
        second = total[spill + block : spill + 3 * block, : strips * block]
        chosen = jnp.where(band == 0, first, second).astype(jnp.bfloat16)
        rows_ref[k * 2 * block : (k + 1) * 2 * block, :] = chosen
        cols = both.astype(jnp.float32)
        left = jnp.where(lane_e < block, 0.0, cols[out_rows - spill :])
        right = jnp.where(lane_e < block, pltpu.roll(cols[:spill], block, 1), 0.0)
        both_edges = jnp.concatenate([left, right], axis=0)
        edge_ref[:, k * LANES : (k + 1) * LANES] = both_edges.astype(jnp.bfloat16)
        cols = jnp.concatenate([cols, jnp.zeros((LANES - out_rows, LANES), jnp.float32)], axis=0)
        turned = cols.T[block:, :]
        turned = jnp.concatenate([turned, jnp.zeros_like(turned)], axis=1)
        for b in range(4):
            shift = (b * block - spill) % (2 * LANES)
            placed = pltpu.roll(turned, shift, 1)
            kept = placed
            if b == 0:
                kept = jnp.where(lane_c < 2 * LANES - spill, placed, 0.0)
            if b == 3:
                kept = jnp.where(lane_c >= spill, placed, 0.0)
            at = k * 4 * block + b * block
            main_ref[at : at + block, :] = kept.astype(jnp.bfloat16)
    deep = tall - share * out_rows
    row = lax.broadcasted_iota(jnp.int32, (kinds, sources * deep), 0)
    col = lax.broadcasted_iota(jnp.int32, (kinds, sources * deep), 1)
    core = jnp.where(row < share * sources, band, 1 - band)
    wanted = row // share % sources * deep + core * share + row % share
    find = jnp.where(col == wanted, 1.0, 0.0).astype(jnp.bfloat16)
    pair = []
    for stack in stacks:
        lines = [stack[(s + 1) * tall - deep : (s + 1) * tall, :] for s in range(sources)]
        lines = jnp.concatenate(lines, axis=0)
        pair.append(jnp.dot(find, lines, preferred_element_type=jnp.float32))
    table = [jnp.where(band == b, pair[0], pair[1]).astype(jnp.bfloat16) for b in range(2)]
    table = jnp.concatenate(table, axis=1)
    src = lax.broadcasted_iota(jnp.int32, (table.shape[1], col_grid * block), 0)
    dst = lax.broadcasted_iota(jnp.int32, (table.shape[1], col_grid * block), 1)
    ahead = src - dst // block
    first_exp = lax.axis_index("basis") * exp_local
    exp_group = group_blocks // per_exp
    for x in range(exp_local):
        for s in range(strips):
            block_row = band * (band_grid - 1) + s
            line = (block_row // band_grid * exp_group + first_exp + x) * band_grid + block_row % band_grid
            spread = jnp.where(ahead == line * col_grid, 1.0, 0.0).astype(jnp.bfloat16)
            lines = jnp.dot(table, spread, preferred_element_type=jnp.float32)
            for k in range(kinds):
                wide = jnp.broadcast_to(lines[k : k + 1], (16, col_grid * block))
                at = ((x * kinds + k) * strips + s) * 16
                wide_ref[at : at + 16, :] = wide.astype(jnp.bfloat16)


def late_kernel(dims, width, block, kinds, *refs):
    chunks = refs[:-13]
    (pick_ref, before_ref, rows_ref, main_ref, edge_ref, wide_ref, obs_ref, inv_ref, out_ref) = refs[-13:-4]
    sums_ref, image_ref, mid_ref, side_ref = refs[-4:]
    _, _, _, col_grid, band_grid, strips, exp_local, _ = dims
    blocks = exp_local * strips * col_grid
    pitch = sums_ref.shape[0] // (width // LANES)
    summed_into(sums_ref, pick_ref[...], chunks, before_ref, width, blocks, pitch)
    half = block // 2
    low = lax.broadcasted_iota(jnp.int32, (half, LANES), 1) < block
    tall = strips * block
    window = 4 * block
    band_rows = band_grid * block
    low_band = lax.broadcasted_iota(jnp.int32, (band_rows, LANES), 1) < block

    def laid_out(x, s, m):
        n = (x * strips + s) * col_grid + 2 * m
        a = sums_ref[pl.ds(n, half, stride=pitch), :]
        b = sums_ref[pl.ds(n + 1, half, stride=pitch), :]
        even = jnp.where(low, a, pltpu.roll(b, block, 1))
        odd = jnp.where(low, pltpu.roll(a, block, 1), b)
        at = s * block
        cols = slice(m * LANES, (m + 1) * LANES)
        image_ref[x, at : at + half, cols] = even.astype(jnp.bfloat16)
        image_ref[x, at + half : at + block, cols] = odd.astype(jnp.bfloat16)

    places = [[(x, s, m) for s in range(strips) for m in range(col_grid // 2)] for x in range(exp_local)]
    for place in places[0]:
        laid_out(*place)
    for x in range(exp_local):
        ahead = places[x + 1] if x + 1 < exp_local else []
        for k in range(kinds):
            at = (x * kinds + k) * strips * 16
            rows = rows_ref[k * band_rows : (k + 1) * band_rows, :]
            mids = []
            for w in range(2):
                cols = slice(w * window, (w + 1) * window)
                image = image_ref[x, :, cols].reshape(strips, block // 16, 16, window)
                wide = wide_ref[at : at + strips * 16, cols].reshape(strips, 1, 16, window)
                scaled = (image * wide).reshape(tall, window)
                mid = jnp.dot(rows, scaled, preferred_element_type=jnp.float32)
                top = (w * exp_local + x) * band_rows
                mid_ref[top : top + band_rows, k * window : (k + 1) * window] = mid.astype(jnp.bfloat16)
                mids.append(mid[:, :LANES] if w else mid[:, window - LANES :])
            side = jnp.where(low_band, mids[1], mids[0])
            side_ref[x * band_rows : (x + 1) * band_rows, k * LANES : (k + 1) * LANES] = side.astype(jnp.bfloat16)
            for place in ahead[k :: kinds]:
                laid_out(*place)
    tall2 = exp_local * band_rows
    spill = edge_ref.shape[0] // 2
    side = lax.dot_general(
        edge_ref[...], side_ref[...], (((1,), (1,)), ((), ())), preferred_element_type=jnp.float32
    )
    gap = jnp.zeros((LANES - 2 * spill, tall2), jnp.float32)
    side = jnp.concatenate([side[:spill], gap, side[spill:]], axis=0).T
    low_all = lax.broadcasted_iota(jnp.int32, (tall2, LANES), 1) < block
    mains = jnp.dot(mid_ref[...], main_ref[...], preferred_element_type=jnp.float32)
    for w in range(2):
        main = mains[w * tall2 : (w + 1) * tall2]
        edge = jnp.where(low_all, side, 0.0) if w else jnp.where(low_all, 0.0, side)
        for x in range(exp_local):
            rows = slice(x * band_rows, (x + 1) * band_rows)
            noise = jnp.sqrt(jnp.full((1, LANES), inv_ref[x], jnp.float32))
            for t in range(2):
                model = main[rows, t * LANES : (t + 1) * LANES]
                if t == 1 - w:
                    model = model + edge[rows]
                cols = slice(w * window + t * LANES, w * window + (t + 1) * LANES)
                out_ref[x, :, cols] = noise * (obs_ref[x, :, cols].astype(jnp.float32) - model)


def gathered_device(
    scene_patches, visit_dest, visit_block, row_maps, col_maps, psf_weights, inv_variance, observed
):
    n_exp, n_row, n_basis = (lax.axis_size(a) for a in ("exp", "row", "basis"))
    patch_count, visits = visit_dest.shape
    width = scene_patches.shape[1]
    exp_local, band_rows, tile_cols = observed.shape
    exp_group, kinds_local, band_grid, col_grid = psf_weights.shape
    block = row_maps.shape[2]
    out_width = row_maps.shape[1]
    strips = band_grid + 1
    per_exp = band_grid * col_grid
    group_blocks = exp_group * per_exp
    kinds = kinds_local * n_basis
    basis = lax.axis_index("basis")
    dims = (visits, group_blocks, per_exp, col_grid, band_grid, strips, exp_local, n_row)
    blocks = exp_local * strips * col_grid
    spill = (out_width - block) // 2

    f32, bf16 = jnp.float32, jnp.bfloat16
    params = pltpu.CompilerParams(vmem_limit_bytes=VMEM_BYTES)
    packed = (
        scene_patches,
        visit_dest.T,
        visit_block.T,
        jnp.swapaxes(row_maps, 1, 2),
        jnp.swapaxes(col_maps, 1, 2),
        psf_weights,
    )
    own, row_now, col_now, weights_now = pl.pallas_call(
        pack_kernel,
        out_shape=[
            jax.ShapeDtypeStruct((patch_count, width + LANES), bf16),
            jax.ShapeDtypeStruct((kinds_local, block, out_width), bf16),
            jax.ShapeDtypeStruct((kinds_local, block, out_width), bf16),
            jax.ShapeDtypeStruct(psf_weights.shape, bf16),
        ],
        in_specs=[pl.BlockSpec(memory_space=pltpu.HBM)] * 6,
        out_specs=in_vmem(4),
        scratch_shapes=[pltpu.VMEM((2, visits, patch_count), jnp.int32), pltpu.SemaphoreType.DMA((6,))],
        compiler_params=params,
    )(*(pltpu.with_memory_space_constraint(v, pltpu.HBM) for v in packed))
    part = patch_count // n_basis
    own_part = lax.dynamic_slice_in_dim(own, basis * part, part, 0)
    far = []
    for s in range(2, n_exp):
        far.append(swapped(own_part, "exp", s))
    maps = pl.pallas_call(
        parcel_kernel,
        out_shape=jax.ShapeDtypeStruct((kinds_local // n_row * out_width, LANES), bf16),
        in_specs=in_vmem(2),
        out_specs=in_vmem(1)[0],
        compiler_params=params,
    )(row_now, col_now)
    table = jnp.swapaxes(weights_now, 0, 1).reshape(kinds_local, -1)
    table = jnp.pad(table, ((0, 16 - kinds_local), (0, 0)))
    maps = jnp.concatenate([maps, table], axis=0)
    parcels = [maps]
    for s in range(1, n_basis):
        parcels.append(swapped(maps, "basis", s))
    near = swapped(own, "exp", 1)
    bare = jnp.concatenate([v[:, :width] for v in far], axis=0)
    far = jnp.concatenate(far, axis=0)
    spread = []
    for s in range(n_basis - 1, 0, -1):
        spread.append(swapped(bare, "basis", s))
    own_other = swapped(own, "row", 1)
    far_other = swapped(far, "row", 1)
    stack = pl.pallas_call(
        stack_kernel,
        out_shape=jax.ShapeDtypeStruct((n_basis * maps.shape[0], LANES), bf16),
        in_specs=in_vmem(n_basis),
        out_specs=in_vmem(1)[0],
        compiler_params=params,
    )(*parcels)
    stack_other = swapped(stack, "row", 1)
    near_other = swapped(near, "row", 1)
    spread_other = []
    for s, v in zip(range(n_basis - 1, 0, -1), spread):
        spread_other.append(swapped(v, "row", 1))

    early = [own, far, own_other, far_other, stack, stack_other]
    shapes = [
        jax.ShapeDtypeStruct((width // LANES * blocks, LANES), f32),
        jax.ShapeDtypeStruct((kinds * band_rows, strips * block), bf16),
        jax.ShapeDtypeStruct((kinds * 4 * block, 4 * block), bf16),
        jax.ShapeDtypeStruct((2 * spill, kinds * LANES), bf16),
        jax.ShapeDtypeStruct((exp_local * kinds * strips * 16, tile_cols), bf16),
    ]
    early_call = pl.pallas_call(
        functools.partial(early_kernel, dims, width, block, kinds, n_basis),
        out_shape=shapes,
        in_specs=in_vmem(len(early)),
        out_specs=in_vmem(len(shapes)),
        compiler_params=params,
    )
    prepared = early_call(*early)
    late_count = 2 * (patch_count + (n_basis - 1) * far.shape[0])
    pick = pl.pallas_call(
        functools.partial(pick_kernel, dims, width, n_basis),
        out_shape=jax.ShapeDtypeStruct((blocks, late_count), bf16),
        in_specs=in_vmem(4),
        out_specs=in_vmem(1)[0],
        compiler_params=params,
    )(near, near_other, far, far_other)
    late = [near, near_other] + spread + spread_other + [pick] + list(prepared) + [observed]
    return pl.pallas_call(
        functools.partial(late_kernel, dims, width, block, kinds),
        out_shape=jax.ShapeDtypeStruct(observed.shape, f32),
        in_specs=in_vmem(len(late)) + [pl.BlockSpec(memory_space=pltpu.SMEM)],
        out_specs=pl.BlockSpec(memory_space=pltpu.VMEM),
        scratch_shapes=[
            pltpu.VMEM((width // LANES * (blocks + ROW_PAD), LANES), f32),
            pltpu.VMEM((exp_local, strips * block, tile_cols), bf16),
            pltpu.VMEM((2 * exp_local * band_rows, kinds * 4 * block), bf16),
            pltpu.VMEM((exp_local * band_rows, kinds * LANES), bf16),
        ],
        compiler_params=params,
    )(*late, inv_variance)


def passed_along(value, axis, by):
    length = lax.axis_size(axis)
    pairs = [(i, i + by) for i in range(length) if 0 <= i + by < length]
    return lax.ppermute(value, axis, pairs)


def pad_last(values, lower, upper):
    widths = [(0, 0)] * (values.ndim - 1) + [(lower, upper)]
    return jnp.pad(values, widths)


def fold_last(values, block_size):
    blocks_along = values.shape[-2]
    edge_width = values.shape[-1] - block_size
    lead = values.shape[:-2]
    head_part = values[..., :block_size].reshape(lead + (blocks_along * block_size,))
    tail_part = pad_last(values[..., block_size:], 0, block_size - edge_width)
    tail_part = tail_part.reshape(lead + (blocks_along * block_size,))
    head_part = pad_last(head_part, 0, edge_width)
    tail_part = pad_last(tail_part, block_size, 0)[..., : blocks_along * block_size + edge_width]
    return head_part + tail_part


def fold_blocks(images, block_size):
    images = jnp.swapaxes(images, -3, -2)
    images = fold_last(images, block_size)
    images = jnp.moveaxis(images, -1, -3)
    images = fold_last(images, block_size)
    return jnp.swapaxes(images, -1, -2)


def band_model(block_rows, weights, row_ops, col_ops, spill_rows, tile_cols):
    count_exp, kind_count, block_grid, col_grid = weights.shape
    block_size = row_ops.shape[2]
    out_width = row_ops.shape[1]
    tile_blocks = block_rows.reshape(-1, block_size, block_size)
    smeared = jnp.einsum(
        "nij,kcj->knic", tile_blocks, col_ops, preferred_element_type=jnp.float32
    ).astype(jnp.bfloat16)
    smeared = lax.optimization_barrier(smeared)
    scales = jnp.swapaxes(weights, 0, 1).reshape(kind_count, -1).astype(jnp.float32)
    scaled = (scales[:, :, None, None] * smeared).astype(jnp.bfloat16)
    images = jnp.einsum("kor,knrc->noc", row_ops, scaled, preferred_element_type=jnp.float32)
    images = images.reshape(count_exp, block_grid, col_grid, out_width, out_width)
    canvas = fold_blocks(images, block_size)
    return canvas[:, :, spill_rows : spill_rows + tile_cols]


def exchanged_device(
    scene_patches, visit_dest, visit_block, row_maps, col_maps, psf_weights, inv_variance, observed
):
    group_size = lax.axis_size("exp") * lax.axis_size("row")
    patch_count, visit_count = visit_dest.shape
    capacity = max(2, 2 * patch_count * visit_count // group_size)
    exp_local, band_rows, tile_cols = observed.shape
    _, _, block_grid, col_grid = psf_weights.shape
    block_size = row_maps.shape[2]
    spill_rows = (row_maps.shape[1] - block_size) // 2
    per_exposure = block_grid * col_grid
    flat_dest = visit_dest.reshape(-1)
    matches = (flat_dest[:, None] == jnp.arange(group_size, dtype=jnp.int32)[None, :]).astype(
        jnp.int32
    )
    slot_rank = jnp.sum(jnp.cumsum(matches, axis=0) * matches, axis=1) - 1
    slot_index = flat_dest * capacity + slot_rank
    select_mat = (
        slot_index[None, :] == jnp.arange(group_size * capacity, dtype=jnp.int32)[:, None]
    ).astype(jnp.int32)
    tagged = jnp.sum(select_mat * (visit_block.reshape(-1) + 1)[None, :], axis=1).astype(
        jnp.bfloat16
    )
    picker = jnp.sum(
        select_mat.reshape(group_size * capacity, patch_count, visit_count), axis=2
    ).astype(jnp.bfloat16)
    outgoing = jnp.dot(picker, scene_patches, preferred_element_type=jnp.float32).astype(
        jnp.bfloat16
    )
    shaped = outgoing.reshape(group_size, capacity, -1)
    labels = tagged.reshape(group_size, capacity)
    arrived, arrived_tags = (
        lax.all_to_all(shaped, ("exp", "row"), split_axis=0, concat_axis=0, tiled=True),
        lax.all_to_all(labels, ("exp", "row"), split_axis=0, concat_axis=0, tiled=True),
    )
    arrived = arrived.reshape(group_size * capacity, -1)
    arrived_tags = arrived_tags.reshape(-1).astype(jnp.int32)
    row_all, col_all, weight_all = (
        lax.all_gather(row_maps, "basis", axis=0, tiled=True),
        lax.all_gather(col_maps, "basis", axis=0, tiled=True),
        lax.all_gather(psf_weights, "basis", axis=1, tiled=True),
    )
    first_exp = lax.axis_index("basis") * exp_local
    wanted = first_exp * per_exposure + 1 + jnp.arange(exp_local * per_exposure, dtype=jnp.int32)
    placing = (arrived_tags[None, :] == wanted[:, None]).astype(jnp.bfloat16)
    own_blocks = jnp.dot(placing, arrived, preferred_element_type=jnp.float32).astype(jnp.bfloat16)
    own_weights = lax.dynamic_slice_in_dim(weight_all, first_exp, exp_local, 0)
    model_band = band_model(own_blocks, own_weights, row_all, col_all, spill_rows, tile_cols)
    upper_spill = model_band[:, :spill_rows]
    lower_spill = model_band[:, spill_rows + band_rows :]
    from_above = passed_along(lower_spill.astype(jnp.bfloat16), "row", 1).astype(lower_spill.dtype)
    from_below = passed_along(upper_spill.astype(jnp.bfloat16), "row", -1).astype(upper_spill.dtype)
    core_rows = model_band[:, spill_rows : spill_rows + band_rows]
    core_rows = core_rows.at[:, :spill_rows].add(from_above)
    core_rows = core_rows.at[:, band_rows - spill_rows :].add(from_below)
    return jnp.sqrt(inv_variance)[:, None, None] * (observed.astype(jnp.float32) - core_rows)


def gathers(mesh, patch_count, visits):
    n_exp, n_row, n_basis = mesh.shape["exp"], mesh.shape["row"], mesh.shape["basis"]
    capacity = max(2, 2 * patch_count * visits // (n_exp * n_row))
    powers = all(n & (n - 1) == 0 for n in (n_exp, n_basis)) and n_exp > 2 and n_basis > 2
    return capacity >= patch_count and powers and n_row == 2 and patch_count % (8 * n_basis) == 0


def in_layer(*arrays):
    return gathered_device(*arrays)


def solution(mesh):
    def step(*arrays):
        patch_total, visits = arrays[1].shape
        patch_count = patch_total // (mesh.shape["exp"] * mesh.shape["row"])
        gather = gathers(mesh, patch_count, visits)
        sharded = jax.shard_map(
            in_layer if gather else exchanged_device,
            mesh=mesh,
            in_specs=(
                P(("exp", "row"), None),
                P(("exp", "row"), None),
                P(("exp", "row"), None),
                P("basis", None, None),
                P("basis", None, None),
                P("exp", "basis", "row", None),
                P(("exp", "basis")),
                P(("exp", "basis"), "row", None),
            ),
            out_specs=P(("exp", "basis"), "row", None),
            check_vma=False,
        )
        return sharded(*arrays)

    return step
```

```python
import functools
import jax
import jax.numpy as jnp
from jax import lax
from jax.experimental import pallas as pl
from jax.experimental.pallas import tpu as pltpu
from jax.sharding import PartitionSpec as P


LANES = 128
TAGS_AT = 64
ROW_PAD = 4
VMEM_BYTES = 28 * 1024 * 1024


def swapped(value, axis, by):
    length = lax.axis_size(axis)
    return lax.ppermute(value, axis, [(i, i ^ by) for i in range(length)])


def in_vmem(count):
    return [pl.BlockSpec(memory_space=pltpu.VMEM)] * count


def pack_kernel(patch_ref, dest_ref, block_ref, row_ref, col_ref, weight_ref, *refs):
    own_ref, row_out, col_out, weight_out, tag_buf, sems = refs
    width = patch_ref.shape[1]
    patch_count = patch_ref.shape[0]
    visits = dest_ref.shape[0]
    pairs = (
        (dest_ref, tag_buf.at[0]),
        (block_ref, tag_buf.at[1]),
        (patch_ref, own_ref.at[:, :width]),
        (row_ref, row_out),
        (col_ref, col_out),
        (weight_ref, weight_out),
    )
    copies = [pltpu.make_async_copy(src, dst, sems.at[i]) for i, (src, dst) in enumerate(pairs)]
    for copy in copies:
        copy.start()
    copies[0].wait()
    copies[1].wait()
    tags = jnp.concatenate([tag_buf[0], tag_buf[1]], axis=0).astype(jnp.float32)
    tags = jnp.concatenate([tags, jnp.zeros((2 * visits, LANES - patch_count), jnp.float32)], axis=1)
    tags = jnp.concatenate([tags, jnp.zeros((LANES - 2 * visits, LANES), jnp.float32)], axis=0)
    tags = tags.T[:patch_count]
    part = patch_count // lax.axis_size("basis")
    pieces = [tags[at : at + part] for at in range(0, patch_count, part)]
    every = pieces[0]
    for i, piece in enumerate(pieces[1:], 1):
        every = every + pltpu.roll(piece, 2 * visits * i, 1)
    tags = jnp.concatenate([every + pltpu.roll(piece, TAGS_AT, 1) for piece in pieces], axis=0)
    own_ref[:, width:] = tags.astype(jnp.bfloat16)
    for copy in copies[2:]:
        copy.wait()


def parcel_kernel(row_ref, col_ref, maps_ref):
    kinds_local, _, rows = row_ref.shape
    share = kinds_local // lax.axis_size("row")
    first = lax.axis_index("row") * share
    for i in range(share):
        both = [ref[first + i].astype(jnp.float32) for ref in (row_ref, col_ref)]
        both = jnp.concatenate(both, axis=0)
        both = jnp.concatenate([both, jnp.zeros((LANES, LANES - rows), jnp.float32)], axis=1)
        maps_ref[i * rows : (i + 1) * rows, :] = both.T[:rows].astype(jnp.bfloat16)


def stack_kernel(*refs):
    *parts, out_ref = refs
    at = 0
    for part in parts:
        out_ref[at : at + part.shape[0], :] = part[...]
        at += part.shape[0]


def picks(tags, dims):
    visits, group_blocks, per_exp, col_grid, band_grid, strips, exp_local, rows_axis = dims
    group, band, basis = lax.axis_index("exp"), lax.axis_index("row"), lax.axis_index("basis")
    codes = tags[:, :visits] * group_blocks + tags[:, visits : 2 * visits]
    lane = lax.broadcasted_iota(jnp.int32, (1, LANES), 1)
    exp_at = lane // (strips * col_grid)
    strip = lane // col_grid % strips
    block_row = band * (band_grid - 1) + strip
    dest = group * rows_axis + block_row // band_grid
    block = (basis * exp_local + exp_at) * per_exp + block_row % band_grid * col_grid + lane % col_grid
    want = jnp.where(exp_at < exp_local, dest * group_blocks + block, -1).astype(jnp.float32)
    hit = jnp.zeros((tags.shape[0], LANES), jnp.float32)
    for v in range(visits):
        hit = hit + jnp.where(codes[:, v : v + 1] == want, 1.0, 0.0)
    return hit.T[: exp_local * strips * col_grid].astype(jnp.bfloat16)


def tags_of(ref, width, lane):
    return pltpu.roll(ref[:, width:].astype(jnp.float32), (LANES - lane) % LANES, 1)


def pick_kernel(dims, width, sources, near_ref, near_other_ref, far_ref, far_other_ref, pick_ref):
    tags = [tags_of(ref, width, TAGS_AT) for ref in (near_ref, near_other_ref)]
    basis = lax.axis_index("basis")
    for ref in (far_ref, far_other_ref):
        tags += [tags_of(ref, width, (basis ^ s) * 2 * dims[0]) for s in range(sources - 1, 0, -1)]
    pick_ref[...] = picks(jnp.concatenate(tags, axis=0), dims)


def summed_into(out_ref, pick, chunk_refs, before_ref, width, blocks, pitch):
    step = 4 * LANES
    for start in range(0, width, step):
        rows = jnp.concatenate([ref[:, start : start + step] for ref in chunk_refs], axis=0)
        part = jnp.dot(pick, rows, preferred_element_type=jnp.float32)
        for t in range(step // LANES):
            at = (start // LANES + t) * blocks
            piece = part[:, t * LANES : (t + 1) * LANES]
            if before_ref is not None:
                piece = piece + before_ref[at : at + blocks, :]
            at = (start // LANES + t) * pitch
            out_ref[at : at + blocks, :] = piece


def early_kernel(dims, width, block, kinds, sources, *refs):
    chunks, stacks = refs[:4], refs[4:6]
    sums_ref, rows_ref, main_ref, edge_ref, wide_ref = refs[-5:]
    _, group_blocks, per_exp, col_grid, band_grid, strips, exp_local, _ = dims
    blocks = exp_local * strips * col_grid
    tags = jnp.concatenate([tags_of(ref, width, TAGS_AT) for ref in chunks], axis=0)
    summed_into(sums_ref, picks(tags, dims), chunks, None, width, blocks, blocks)
    band = lax.axis_index("row")
    out_rows = 96
    share = kinds // (2 * sources)
    tall = stacks[0].shape[0] // sources
    src = lax.broadcasted_iota(jnp.int32, (LANES, 2 * LANES), 0)
    dst = lax.broadcasted_iota(jnp.int32, (LANES, 2 * LANES), 1)
    half = block // 2
    inner = dst % block
    wanted = inner % half * 2 + inner // half
    perm = jnp.where((src == wanted) & (dst < strips * block), 1.0, 0.0).astype(jnp.bfloat16)
    lane2 = lax.broadcasted_iota(jnp.int32, (out_rows, 2 * LANES), 1)
    spill = (out_rows - block) // 2
    lane_c = lax.broadcasted_iota(jnp.int32, (block, 2 * LANES), 1)
    lane_e = lax.broadcasted_iota(jnp.int32, (spill, LANES), 1)
    for k in range(kinds):
        at = k // share % sources * tall + k % share * out_rows
        both = stacks[k // (share * sources)][at : at + out_rows, :]
        moved = jnp.dot(both, perm, preferred_element_type=jnp.float32)
        gap = jnp.zeros((block, 2 * LANES), jnp.float32)
        total = None
        for s in range(strips):
            piece = jnp.where(lane2 // block == s, moved, 0.0)
            parts = [gap] * s + [piece] + [gap] * (strips - 1 - s)
            piece = jnp.concatenate(parts, axis=0)
            total = piece if total is None else total + piece
        first = total[spill : spill + 2 * block, : strips * block]
        second = total[spill + block : spill + 3 * block, : strips * block]
        chosen = jnp.where(band == 0, first, second).astype(jnp.bfloat16)
        rows_ref[k * 2 * block : (k + 1) * 2 * block, :] = chosen
        cols = both.astype(jnp.float32)
        left = jnp.where(lane_e < block, 0.0, cols[out_rows - spill :])
        right = jnp.where(lane_e < block, pltpu.roll(cols[:spill], block, 1), 0.0)
        both_edges = jnp.concatenate([left, right], axis=0)
        edge_ref[:, k * LANES : (k + 1) * LANES] = both_edges.astype(jnp.bfloat16)
        cols = jnp.concatenate([cols, jnp.zeros((LANES - out_rows, LANES), jnp.float32)], axis=0)
        turned = cols.T[block:, :]
        turned = jnp.concatenate([turned, jnp.zeros_like(turned)], axis=1)
        for b in range(4):
            shift = (b * block - spill) % (2 * LANES)
            placed = pltpu.roll(turned, shift, 1)
            kept = placed
            if b == 0:
                kept = jnp.where(lane_c < 2 * LANES - spill, placed, 0.0)
            if b == 3:
                kept = jnp.where(lane_c >= spill, placed, 0.0)
            at = k * 4 * block + b * block
            main_ref[at : at + block, :] = kept.astype(jnp.bfloat16)
    deep = tall - share * out_rows
    row = lax.broadcasted_iota(jnp.int32, (kinds, sources * deep), 0)
    col = lax.broadcasted_iota(jnp.int32, (kinds, sources * deep), 1)
    core = jnp.where(row < share * sources, band, 1 - band)
    wanted = row // share % sources * deep + core * share + row % share
    find = jnp.where(col == wanted, 1.0, 0.0).astype(jnp.bfloat16)
    pair = []
    for stack in stacks:
        lines = [stack[(s + 1) * tall - deep : (s + 1) * tall, :] for s in range(sources)]
        lines = jnp.concatenate(lines, axis=0)
        pair.append(jnp.dot(find, lines, preferred_element_type=jnp.float32))
    table = [jnp.where(band == b, pair[0], pair[1]).astype(jnp.bfloat16) for b in range(2)]
    table = jnp.concatenate(table, axis=1)
    src = lax.broadcasted_iota(jnp.int32, (table.shape[1], col_grid * block), 0)
    dst = lax.broadcasted_iota(jnp.int32, (table.shape[1], col_grid * block), 1)
    ahead = src - dst // block
    first_exp = lax.axis_index("basis") * exp_local
    exp_group = group_blocks // per_exp
    for x in range(exp_local):
        for s in range(strips):
            block_row = band * (band_grid - 1) + s
            line = (block_row // band_grid * exp_group + first_exp + x) * band_grid + block_row % band_grid
            spread = jnp.where(ahead == line * col_grid, 1.0, 0.0).astype(jnp.bfloat16)
            lines = jnp.dot(table, spread, preferred_element_type=jnp.float32)
            for k in range(kinds):
                wide = jnp.broadcast_to(lines[k : k + 1], (16, col_grid * block))
                at = ((x * kinds + k) * strips + s) * 16
                wide_ref[at : at + 16, :] = wide.astype(jnp.bfloat16)


def late_kernel(dims, width, block, kinds, *refs):
    chunks = refs[:-15]
    (pick_ref, before_ref, rows_ref, main_ref, edge_ref, wide_ref, obs_ref, inv_ref, out_ref) = refs[-15:-6]
    sums_ref, image_ref, mid_ref, side_ref, out_buf, out_sems = refs[-6:]
    _, _, _, col_grid, band_grid, strips, exp_local, _ = dims
    blocks = exp_local * strips * col_grid
    pitch = sums_ref.shape[0] // (width // LANES)
    summed_into(sums_ref, pick_ref[...], chunks, before_ref, width, blocks, pitch)
    half = block // 2
    low = lax.broadcasted_iota(jnp.int32, (half, LANES), 1) < block
    tall = strips * block
    window = 4 * block
    band_rows = band_grid * block
    low_band = lax.broadcasted_iota(jnp.int32, (band_rows, LANES), 1) < block

    def laid_out(x, s, m):
        n = (x * strips + s) * col_grid + 2 * m
        a = sums_ref[pl.ds(n, half, stride=pitch), :]
        b = sums_ref[pl.ds(n + 1, half, stride=pitch), :]
        even = jnp.where(low, a, pltpu.roll(b, block, 1))
        odd = jnp.where(low, pltpu.roll(a, block, 1), b)
        at = s * block
        cols = slice(m * LANES, (m + 1) * LANES)
        image_ref[x, at : at + half, cols] = even.astype(jnp.bfloat16)
        image_ref[x, at + half : at + block, cols] = odd.astype(jnp.bfloat16)

    places = [[(x, s, m) for s in range(strips) for m in range(col_grid // 2)] for x in range(exp_local)]
    for place in places[0]:
        laid_out(*place)
    for x in range(exp_local):
        ahead = places[x + 1] if x + 1 < exp_local else []
        for k in range(kinds):
            at = (x * kinds + k) * strips * 16
            rows = rows_ref[k * band_rows : (k + 1) * band_rows, :]
            mids = []
            for w in range(2):
                cols = slice(w * window, (w + 1) * window)
                image = image_ref[x, :, cols].reshape(strips, block // 16, 16, window)
                wide = wide_ref[at : at + strips * 16, cols].reshape(strips, 1, 16, window)
                scaled = (image * wide).reshape(tall, window)
                mid = jnp.dot(rows, scaled, preferred_element_type=jnp.float32)
                top = (w * exp_local + x) * band_rows
                mid_ref[top : top + band_rows, k * window : (k + 1) * window] = mid.astype(jnp.bfloat16)
                mids.append(mid[:, :LANES] if w else mid[:, window - LANES :])
            side = jnp.where(low_band, mids[1], mids[0])
            side_ref[x * band_rows : (x + 1) * band_rows, k * LANES : (k + 1) * LANES] = side.astype(jnp.bfloat16)
            for place in ahead[k :: kinds]:
                laid_out(*place)
    tall2 = exp_local * band_rows
    spill = edge_ref.shape[0] // 2
    side = lax.dot_general(
        edge_ref[...], side_ref[...], (((1,), (1,)), ((), ())), preferred_element_type=jnp.float32
    )
    gap = jnp.zeros((LANES - 2 * spill, tall2), jnp.float32)
    side = jnp.concatenate([side[:spill], gap, side[spill:]], axis=0).T
    copies = []
    low_all = lax.broadcasted_iota(jnp.int32, (tall2, LANES), 1) < block
    mains = jnp.dot(mid_ref[...], main_ref[...], preferred_element_type=jnp.float32)
    for w in range(2):
        main = mains[w * tall2 : (w + 1) * tall2]
        edge = jnp.where(low_all, side, 0.0) if w else jnp.where(low_all, 0.0, side)
        for x in range(exp_local):
            rows = slice(x * band_rows, (x + 1) * band_rows)
            noise = jnp.sqrt(jnp.full((1, LANES), inv_ref[x], jnp.float32))
            for t in range(2):
                model = main[rows, t * LANES : (t + 1) * LANES]
                if t == 1 - w:
                    model = model + edge[rows]
                cols = slice(w * window + t * LANES, w * window + (t + 1) * LANES)
                out_buf[x, :, cols] = noise * (obs_ref[x, :, cols].astype(jnp.float32) - model)
            cols = slice(w * window, (w + 1) * window)
            copy = pltpu.make_async_copy(out_buf.at[x, :, cols], out_ref.at[x, :, cols], out_sems.at[w, x])
            copy.start()
            copies.append(copy)
    for copy in copies:
        copy.wait()


def gathered_device(
    scene_patches, visit_dest, visit_block, row_maps, col_maps, psf_weights, inv_variance, observed
):
    n_exp, n_row, n_basis = (lax.axis_size(a) for a in ("exp", "row", "basis"))
    patch_count, visits = visit_dest.shape
    width = scene_patches.shape[1]
    exp_local, band_rows, tile_cols = observed.shape
    exp_group, kinds_local, band_grid, col_grid = psf_weights.shape
    block = row_maps.shape[2]
    out_width = row_maps.shape[1]
    strips = band_grid + 1
    per_exp = band_grid * col_grid
    group_blocks = exp_group * per_exp
    kinds = kinds_local * n_basis
    basis = lax.axis_index("basis")
    dims = (visits, group_blocks, per_exp, col_grid, band_grid, strips, exp_local, n_row)
    blocks = exp_local * strips * col_grid
    spill = (out_width - block) // 2

    f32, bf16 = jnp.float32, jnp.bfloat16
    params = pltpu.CompilerParams(vmem_limit_bytes=VMEM_BYTES)
    packed = (
        scene_patches,
        visit_dest.T,
        visit_block.T,
        jnp.swapaxes(row_maps, 1, 2),
        jnp.swapaxes(col_maps, 1, 2),
        psf_weights,
    )
    own, row_now, col_now, weights_now = pl.pallas_call(
        pack_kernel,
        out_shape=[
            jax.ShapeDtypeStruct((patch_count, width + LANES), bf16),
            jax.ShapeDtypeStruct((kinds_local, block, out_width), bf16),
            jax.ShapeDtypeStruct((kinds_local, block, out_width), bf16),
            jax.ShapeDtypeStruct(psf_weights.shape, bf16),
        ],
        in_specs=[pl.BlockSpec(memory_space=pltpu.HBM)] * 6,
        out_specs=in_vmem(4),
        scratch_shapes=[pltpu.VMEM((2, visits, patch_count), jnp.int32), pltpu.SemaphoreType.DMA((6,))],
        compiler_params=params,
    )(*(pltpu.with_memory_space_constraint(v, pltpu.HBM) for v in packed))
    part = patch_count // n_basis
    own_part = lax.dynamic_slice_in_dim(own, basis * part, part, 0)
    far = []
    for s in range(2, n_exp):
        far.append(swapped(own_part, "exp", s))
    maps = pl.pallas_call(
        parcel_kernel,
        out_shape=jax.ShapeDtypeStruct((kinds_local // n_row * out_width, LANES), bf16),
        in_specs=in_vmem(2),
        out_specs=in_vmem(1)[0],
        compiler_params=params,
    )(row_now, col_now)
    table = jnp.swapaxes(weights_now, 0, 1).reshape(kinds_local, -1)
    table = jnp.pad(table, ((0, 16 - kinds_local), (0, 0)))
    maps = jnp.concatenate([maps, table], axis=0)
    parcels = [maps]
    for s in range(1, n_basis):
        parcels.append(swapped(maps, "basis", s))
    near = swapped(own, "exp", 1)
    bare = jnp.concatenate([v[:, :width] for v in far], axis=0)
    far = jnp.concatenate(far, axis=0)
    spread = []
    for s in range(n_basis - 1, 0, -1):
        spread.append(swapped(bare, "basis", s))
    own_other = swapped(own, "row", 1)
    far_other = swapped(far, "row", 1)
    stack = pl.pallas_call(
        stack_kernel,
        out_shape=jax.ShapeDtypeStruct((n_basis * maps.shape[0], LANES), bf16),
        in_specs=in_vmem(n_basis),
        out_specs=in_vmem(1)[0],
        compiler_params=params,
    )(*parcels)
    stack_other = swapped(stack, "row", 1)
    near_other = swapped(near, "row", 1)
    spread_other = []
    for s, v in zip(range(n_basis - 1, 0, -1), spread):
        spread_other.append(swapped(v, "row", 1))

    early = [own, far, own_other, far_other, stack, stack_other]
    shapes = [
        jax.ShapeDtypeStruct((width // LANES * blocks, LANES), f32),
        jax.ShapeDtypeStruct((kinds * band_rows, strips * block), bf16),
        jax.ShapeDtypeStruct((kinds * 4 * block, 4 * block), bf16),
        jax.ShapeDtypeStruct((2 * spill, kinds * LANES), bf16),
        jax.ShapeDtypeStruct((exp_local * kinds * strips * 16, tile_cols), bf16),
    ]
    early_call = pl.pallas_call(
        functools.partial(early_kernel, dims, width, block, kinds, n_basis),
        out_shape=shapes,
        in_specs=in_vmem(len(early)),
        out_specs=in_vmem(len(shapes)),
        compiler_params=params,
    )
    prepared = early_call(*early)
    late_count = 2 * (patch_count + (n_basis - 1) * far.shape[0])
    pick = pl.pallas_call(
        functools.partial(pick_kernel, dims, width, n_basis),
        out_shape=jax.ShapeDtypeStruct((blocks, late_count), bf16),
        in_specs=in_vmem(4),
        out_specs=in_vmem(1)[0],
        compiler_params=params,
    )(near, near_other, far, far_other)
    late = [near, near_other] + spread + spread_other + [pick] + list(prepared) + [observed]
    return pl.pallas_call(
        functools.partial(late_kernel, dims, width, block, kinds),
        out_shape=jax.ShapeDtypeStruct(observed.shape, f32),
        in_specs=in_vmem(len(late)) + [pl.BlockSpec(memory_space=pltpu.SMEM)],
        out_specs=pl.BlockSpec(memory_space=pltpu.HBM),
        scratch_shapes=[
            pltpu.VMEM((width // LANES * (blocks + ROW_PAD), LANES), f32),
            pltpu.VMEM((exp_local, strips * block, tile_cols), bf16),
            pltpu.VMEM((2 * exp_local * band_rows, kinds * 4 * block), bf16),
            pltpu.VMEM((exp_local * band_rows, kinds * LANES), bf16),
            pltpu.VMEM(observed.shape, f32),
            pltpu.SemaphoreType.DMA((2, exp_local)),
        ],
        compiler_params=params,
    )(*late, inv_variance)


def passed_along(value, axis, by):
    length = lax.axis_size(axis)
    pairs = [(i, i + by) for i in range(length) if 0 <= i + by < length]
    return lax.ppermute(value, axis, pairs)


def pad_last(values, lower, upper):
    widths = [(0, 0)] * (values.ndim - 1) + [(lower, upper)]
    return jnp.pad(values, widths)


def fold_last(values, block_size):
    blocks_along = values.shape[-2]
    edge_width = values.shape[-1] - block_size
    lead = values.shape[:-2]
    head_part = values[..., :block_size].reshape(lead + (blocks_along * block_size,))
    tail_part = pad_last(values[..., block_size:], 0, block_size - edge_width)
    tail_part = tail_part.reshape(lead + (blocks_along * block_size,))
    head_part = pad_last(head_part, 0, edge_width)
    tail_part = pad_last(tail_part, block_size, 0)[..., : blocks_along * block_size + edge_width]
    return head_part + tail_part


def fold_blocks(images, block_size):
    images = jnp.swapaxes(images, -3, -2)
    images = fold_last(images, block_size)
    images = jnp.moveaxis(images, -1, -3)
    images = fold_last(images, block_size)
    return jnp.swapaxes(images, -1, -2)


def band_model(block_rows, weights, row_ops, col_ops, spill_rows, tile_cols):
    count_exp, kind_count, block_grid, col_grid = weights.shape
    block_size = row_ops.shape[2]
    out_width = row_ops.shape[1]
    tile_blocks = block_rows.reshape(-1, block_size, block_size)
    smeared = jnp.einsum(
        "nij,kcj->knic", tile_blocks, col_ops, preferred_element_type=jnp.float32
    ).astype(jnp.bfloat16)
    smeared = lax.optimization_barrier(smeared)
    scales = jnp.swapaxes(weights, 0, 1).reshape(kind_count, -1).astype(jnp.float32)
    scaled = (scales[:, :, None, None] * smeared).astype(jnp.bfloat16)
    images = jnp.einsum("kor,knrc->noc", row_ops, scaled, preferred_element_type=jnp.float32)
    images = images.reshape(count_exp, block_grid, col_grid, out_width, out_width)
    canvas = fold_blocks(images, block_size)
    return canvas[:, :, spill_rows : spill_rows + tile_cols]


def exchanged_device(
    scene_patches, visit_dest, visit_block, row_maps, col_maps, psf_weights, inv_variance, observed
):
    group_size = lax.axis_size("exp") * lax.axis_size("row")
    patch_count, visit_count = visit_dest.shape
    capacity = max(2, 2 * patch_count * visit_count // group_size)
    exp_local, band_rows, tile_cols = observed.shape
    _, _, block_grid, col_grid = psf_weights.shape
    block_size = row_maps.shape[2]
    spill_rows = (row_maps.shape[1] - block_size) // 2
    per_exposure = block_grid * col_grid
    flat_dest = visit_dest.reshape(-1)
    matches = (flat_dest[:, None] == jnp.arange(group_size, dtype=jnp.int32)[None, :]).astype(
        jnp.int32
    )
    slot_rank = jnp.sum(jnp.cumsum(matches, axis=0) * matches, axis=1) - 1
    slot_index = flat_dest * capacity + slot_rank
    select_mat = (
        slot_index[None, :] == jnp.arange(group_size * capacity, dtype=jnp.int32)[:, None]
    ).astype(jnp.int32)
    tagged = jnp.sum(select_mat * (visit_block.reshape(-1) + 1)[None, :], axis=1).astype(
        jnp.bfloat16
    )
    picker = jnp.sum(
        select_mat.reshape(group_size * capacity, patch_count, visit_count), axis=2
    ).astype(jnp.bfloat16)
    outgoing = jnp.dot(picker, scene_patches, preferred_element_type=jnp.float32).astype(
        jnp.bfloat16
    )
    shaped = outgoing.reshape(group_size, capacity, -1)
    labels = tagged.reshape(group_size, capacity)
    arrived, arrived_tags = (
        lax.all_to_all(shaped, ("exp", "row"), split_axis=0, concat_axis=0, tiled=True),
        lax.all_to_all(labels, ("exp", "row"), split_axis=0, concat_axis=0, tiled=True),
    )
    arrived = arrived.reshape(group_size * capacity, -1)
    arrived_tags = arrived_tags.reshape(-1).astype(jnp.int32)
    row_all, col_all, weight_all = (
        lax.all_gather(row_maps, "basis", axis=0, tiled=True),
        lax.all_gather(col_maps, "basis", axis=0, tiled=True),
        lax.all_gather(psf_weights, "basis", axis=1, tiled=True),
    )
    first_exp = lax.axis_index("basis") * exp_local
    wanted = first_exp * per_exposure + 1 + jnp.arange(exp_local * per_exposure, dtype=jnp.int32)
    placing = (arrived_tags[None, :] == wanted[:, None]).astype(jnp.bfloat16)
    own_blocks = jnp.dot(placing, arrived, preferred_element_type=jnp.float32).astype(jnp.bfloat16)
    own_weights = lax.dynamic_slice_in_dim(weight_all, first_exp, exp_local, 0)
    model_band = band_model(own_blocks, own_weights, row_all, col_all, spill_rows, tile_cols)
    upper_spill = model_band[:, :spill_rows]
    lower_spill = model_band[:, spill_rows + band_rows :]
    from_above = passed_along(lower_spill.astype(jnp.bfloat16), "row", 1).astype(lower_spill.dtype)
    from_below = passed_along(upper_spill.astype(jnp.bfloat16), "row", -1).astype(upper_spill.dtype)
    core_rows = model_band[:, spill_rows : spill_rows + band_rows]
    core_rows = core_rows.at[:, :spill_rows].add(from_above)
    core_rows = core_rows.at[:, band_rows - spill_rows :].add(from_below)
    return jnp.sqrt(inv_variance)[:, None, None] * (observed.astype(jnp.float32) - core_rows)


def gathers(mesh, patch_count, visits):
    n_exp, n_row, n_basis = mesh.shape["exp"], mesh.shape["row"], mesh.shape["basis"]
    capacity = max(2, 2 * patch_count * visits // (n_exp * n_row))
    powers = all(n & (n - 1) == 0 for n in (n_exp, n_basis)) and n_exp > 2 and n_basis > 2
    return capacity >= patch_count and powers and n_row == 2 and patch_count % (8 * n_basis) == 0


def in_layer(*arrays):
    return gathered_device(*arrays)


def solution(mesh):
    def step(*arrays):
        patch_total, visits = arrays[1].shape
        patch_count = patch_total // (mesh.shape["exp"] * mesh.shape["row"])
        gather = gathers(mesh, patch_count, visits)
        sharded = jax.shard_map(
            in_layer if gather else exchanged_device,
            mesh=mesh,
            in_specs=(
                P(("exp", "row"), None),
                P(("exp", "row"), None),
                P(("exp", "row"), None),
                P("basis", None, None),
                P("basis", None, None),
                P("exp", "basis", "row", None),
                P(("exp", "basis")),
                P(("exp", "basis"), "row", None),
            ),
            out_specs=P(("exp", "basis"), "row", None),
            check_vma=False,
        )
        return sharded(*arrays)

    return step
```
